128 devices in a mesh: orbit: 32 (over y, z, core), region: 4 (over x).
Axes of the slice: x: 4, y: 4, z: 4, core: 2. Of those that a mesh axis runs over, the one named last changes fastest.
Arguments:
- footprints: bfloat16 [40960, 64, 256], P(('orbit', 'region')), may hold values from -0.0625 to 0.0625
- block_sounding: int32 [40960], P(('orbit', 'region')), may hold values from 0 to 31
- block_tile: int32 [40960], P(('orbit', 'region')), may hold values from 0 to 31
- block_count: int32 [128], P(('orbit', 'region')), may hold values from 80 to 320, as said below
- observations: float32 [1024, 64, 128], P('orbit'), may hold values from -6 to 6
- obs_weight: float32 [1024, 64], P('orbit'), may hold values from 0.25 to 4
- prior_std: float32 [4, 32, 256], P('region', 'orbit'), may hold values from 0.4 to 4.8
Outputs:
- flux: float32 [4, 32, 256, 128], P('region', 'orbit')
- residual: float32 [4, 32, 256, 128], P('region', 'orbit')
The draws below stay inside these ranges and needn't reach their ends.
Inputs may be any that keep to these rules, and one draw needn't show every extreme that they name: `block_sounding`: index of a sounding block among the 32 of the block's orbit index. `block_tile`: index of a tile among the 32 of the block's region; some tiles are named far more often than others. `block_count`: slots from this count on are unused; some device has all 320 slots live.
All inputs are finite; a program needn't handle non-finite values.
Results may differ from the reference program's by a relative error of at most 0.0068.
Values may be sent and summed in bfloat16 or wider, within the bound.
A program may use at most 128 MiB of HBM per device.

```python
import math
import jax
import jax.numpy as jnp
import numpy as np
from jax import lax

SBLK = 64
CELLS = 256
NRHS = 128
ITERS = 2
NB = 320
SB_DEV = 32
BLOCKS = 40960
SBLOCKS = 1024
TILES_REG = 32
N_ORBIT = 32
N_REGION = 4


def draw_block_count(key, part):
    first_key, second_key = jax.random.split(key)
    devices_all = N_ORBIT * N_REGION
    counts = jax.random.randint(first_key, (devices_all,), NB // 4, NB + 1)
    chosen = jax.random.randint(second_key, (), 0, devices_all)
    return jnp.where(jnp.arange(devices_all) == chosen, NB, counts).astype(jnp.int32)


def draw_prior_std(key, part):
    base = jax.random.uniform(key, (N_REGION, TILES_REG, CELLS), jnp.float32)
    rough = jnp.exp(jnp.log(0.4) + base * jnp.log(4.0))
    place = jnp.arange(N_REGION, dtype=jnp.float32)[:, None] * TILES_REG + jnp.arange(TILES_REG, dtype=jnp.float32)[None, :]
    ramp = 1.0 + 2.0 * place / (N_REGION * TILES_REG - 1)
    return (rough * ramp[:, :, None]).astype(jnp.float32)


def place_ends(entries, stream_key, least, largest):
    spot = [jax.random.randint(jax.random.fold_in(stream_key, axis), (), 0, length) for axis, length in enumerate(entries.shape)]
    longest = entries.shape.index(max(entries.shape))
    beside = spot[:longest] + [(spot[longest] + 1) % entries.shape[longest]] + spot[longest + 1:]
    return entries.at[tuple(spot)].set(least).at[tuple(beside)].set(largest)


def level_of(key, shape, cuts, least, top_value):
    factor_of, own = 1.0, jax.random.fold_in(key, 6)
    for position, shards_of in cuts:
        heights = jnp.exp(jax.random.uniform(jax.random.fold_in(own, position), (shards_of,), jnp.float32, least / len(cuts), top_value / len(cuts)))
        factor_of = factor_of * jnp.repeat(heights, shape[position] // shards_of).reshape([-1 if axis == position else 1 for axis in range(len(shape))])
    return factor_of


def cumulative_ranks(count, lean):
    weights = [(1 << 20) // math.isqrt(rank ** lean) + 1 for rank in range(1, count + 1)]
    scale = 1 + sum(weights) // (1 << 30)
    return np.cumsum(np.array([max(1, weight // scale) for weight in weights]))


def ranked_ids(stream_key, dims, number_of, skew):
    table = cumulative_ranks(number_of, skew)
    pick = jax.random.randint(jax.random.fold_in(stream_key, 1), dims, 0, int(table[number_of - 1]))
    standing = jnp.searchsorted(jnp.asarray(table, jnp.int32), pick, side="right")
    return jax.random.permutation(jax.random.fold_in(stream_key, 2), number_of)[standing].astype(jnp.int32)


def noise(rng, shape, spread, limit, cuts=(), held_as=jnp.bfloat16):
    level = level_of(rng, shape, cuts, -0.22, 0.18) if cuts else 1.0
    array = jax.random.normal(rng, shape, jnp.float32) * spread * level
    return jnp.minimum(jnp.maximum(array, -limit), limit).astype(held_as)


def setup_inputs(seed: int = 0) -> dict:
    streams_of = jax.random.split(jax.random.key(seed), 8)
    footprints = noise(streams_of[0], (BLOCKS, SBLK, CELLS), (CELLS * NB * N_REGION // SB_DEV) ** -0.5, 0.0625, ((0, 128),))
    block_sounding = place_ends(jax.random.randint(streams_of[1], (BLOCKS,), 0, SB_DEV), jax.random.fold_in(streams_of[1], 1), 0, SB_DEV - 1).astype(jnp.int32)
    block_tile = place_ends(ranked_ids(streams_of[2], (BLOCKS,), TILES_REG, 2), jax.random.fold_in(streams_of[2], 3), 0, TILES_REG - 1).astype(jnp.int32)
    block_count = draw_block_count(jax.random.fold_in(streams_of[7], 71), 0)
    observations = noise(streams_of[4], (SBLOCKS, SBLK, NRHS), 1.0, 6.0, ((0, 32),), jnp.float32)
    obs_weight = jnp.clip(jnp.exp(math.log(4.0) - 2.7725887 * jax.random.uniform(streams_of[5], (SBLOCKS, SBLK), jnp.float32) ** level_of(streams_of[5], (SBLOCKS, SBLK), ((0, 32),), -0.2, 0.2)), 0.25, 4.0)
    prior_std = draw_prior_std(jax.random.fold_in(streams_of[7], 71), 0)
    return dict(footprints=footprints, block_sounding=block_sounding, block_tile=block_tile, block_count=block_count, observations=observations, obs_weight=obs_weight, prior_std=prior_std)


def forward_map(footprints, block_sounding, block_tile, block_count, values):
    blocks = footprints.reshape(N_ORBIT * N_REGION, NB, SBLK, CELLS)
    sounds = block_sounding.reshape(N_ORBIT * N_REGION, NB)
    tile_ids = block_tile.reshape(N_ORBIT * N_REGION, NB)
    devices = jnp.arange(N_ORBIT * N_REGION, dtype=jnp.int32)

    def per_device(running, bundle):
        blocks_now, sound_ids, tile_now, live_count, device = bundle
        alive = (jnp.arange(NB) < live_count).astype(jnp.float32)
        region_values = lax.dynamic_index_in_dim(values, device % N_REGION, 0, keepdims=False)
        picked = region_values[tile_now].astype(jnp.float32)
        products = jnp.einsum("bsc,bcr->bsr", blocks_now.astype(jnp.float32), picked) * alive[:, None, None]
        local_sum = jax.ops.segment_sum(products, sound_ids, num_segments=SB_DEV)
        return running.at[device // N_REGION].add(local_sum), None

    start_sum = jnp.zeros((N_ORBIT, SB_DEV, SBLK, NRHS), jnp.float32)
    running, _ = lax.scan(per_device, start_sum, (blocks, sounds, tile_ids, block_count, devices))
    return running


def transpose_map(footprints, block_sounding, block_tile, block_count, weighted):
    blocks = footprints.reshape(N_ORBIT * N_REGION, NB, SBLK, CELLS)
    sounds = block_sounding.reshape(N_ORBIT * N_REGION, NB)
    tile_ids = block_tile.reshape(N_ORBIT * N_REGION, NB)
    devices = jnp.arange(N_ORBIT * N_REGION, dtype=jnp.int32)

    def per_device(running, bundle):
        blocks_now, sound_ids, tile_now, live_count, device = bundle
        alive = (jnp.arange(NB) < live_count).astype(jnp.float32)
        orbit_rows = lax.dynamic_index_in_dim(weighted, device // N_REGION, 0, keepdims=False)
        picked = orbit_rows[sound_ids].astype(jnp.float32)
        contrib = jnp.einsum("bsc,bsr->bcr", blocks_now.astype(jnp.float32), picked) * alive[:, None, None]
        local_sum = jax.ops.segment_sum(contrib, tile_now, num_segments=TILES_REG)
        return running.at[device % N_REGION].add(local_sum), None

    start_sum = jnp.zeros((N_REGION, TILES_REG, CELLS, NRHS), jnp.float32)
    running, _ = lax.scan(per_device, start_sum, (blocks, sounds, tile_ids, block_count, devices))
    return running


def reference(footprints, block_sounding, block_tile, block_count, observations, obs_weight, prior_std):
    weight = obs_weight.reshape(N_ORBIT, SB_DEV, SBLK, 1)
    observed = observations.reshape(N_ORBIT, SB_DEV, SBLK, NRHS)
    prior_scale = prior_std[..., None]
    weighted0 = lax.optimization_barrier((weight * observed).astype(jnp.bfloat16))
    right_side = prior_scale * transpose_map(footprints, block_sounding, block_tile, block_count, weighted0)
    iterate = jnp.zeros_like(right_side)
    residual = right_side
    direction = right_side
    norm_now = jnp.sum(residual * residual, axis=(0, 1, 2))
    for iteration in range(ITERS):
        scaled = lax.optimization_barrier((prior_scale * direction).astype(jnp.bfloat16))
        image = forward_map(footprints, block_sounding, block_tile, block_count, scaled)
        weighted = lax.optimization_barrier((weight * image).astype(jnp.bfloat16))
        product = direction + prior_scale * transpose_map(footprints, block_sounding, block_tile, block_count, weighted)
        step_size = norm_now / jnp.sum(direction * product, axis=(0, 1, 2))
        iterate = iterate + step_size * direction
        residual = residual - step_size * product
        if iteration + 1 < ITERS:
            norm_next = jnp.sum(residual * residual, axis=(0, 1, 2))
            direction = residual + (norm_next / norm_now) * direction
            norm_now = norm_next
    return prior_scale * iterate, residual
```

```python
import functools
import jax
import jax.numpy as jnp
from jax import lax
from jax.experimental import pallas as pl
from jax.experimental.pallas import tpu as pltpu
from jax.sharding import PartitionSpec as P
NB=320; NSLOT=512; GMAX=128; UN=4; RING=16

def prep_kernel(cnt, bt_row, bt_col, bs_col, slots_ref, grp_ref):
    f32=jnp.float32
    n=cnt[0]
    iota=lambda shape,d: lax.broadcasted_iota(jnp.int32, shape, d)
    trow=jnp.where(iota((1,NB),1)<n, bt_row[...], 32)
    live=iota((NB,1),0)<n
    tcol=jnp.where(live, bt_col[...], 32)
    same=(trow==tcol)&(iota((NB,NB),1)<iota((NB,NB),0))
    rank=jnp.sum(jnp.where(same,1.0,0.0),axis=1,keepdims=True)
    lane=iota((NB,128),1)
    num=jnp.sum(jnp.where((tcol==lane)&(lane<32),1.0,0.0),axis=0,keepdims=True)
    g=jnp.floor((num+3.0)*0.25)
    start=jnp.sum(jnp.where(lane<tcol,jnp.broadcast_to(g,(NB,128)),0.0),axis=1,keepdims=True)
    pos=jnp.where(live,4.0*start+rank,-1.0).astype(jnp.int32)
    ident=(iota((NB,1),0)*64+bs_col[...]+1).astype(f32)
    hit=pos==iota((NB,NSLOT),1)
    slots_ref[...]=jnp.sum(jnp.where(hit,jnp.broadcast_to(ident,(NB,NSLOT)),0.0),axis=0,keepdims=True).astype(jnp.int32)
    l2=iota((128,128),1); s2=iota((128,128),0)
    gend=jnp.sum(jnp.where(l2<=s2,jnp.broadcast_to(g,(128,128)),0.0),axis=1,keepdims=True)
    gt=jnp.sum(jnp.where((s2<32)&(gend<=l2.astype(f32)),1.0,0.0),axis=0,keepdims=True)
    total=jnp.sum(g,axis=1,keepdims=True)
    grp_ref[...]=jnp.where(iota((1,128),1)==127,jnp.broadcast_to(total,(1,128)),gt).astype(jnp.int32)

def prep(count, bs, bt):
    return pl.pallas_call(prep_kernel,
        out_shape=(jax.ShapeDtypeStruct((1,NSLOT),jnp.int32),jax.ShapeDtypeStruct((1,128),jnp.int32)),
        in_specs=[pl.BlockSpec(memory_space=pltpu.SMEM)]+[pl.BlockSpec(memory_space=pltpu.VMEM)]*3,
        out_specs=(pl.BlockSpec(memory_space=pltpu.VMEM),)*2,
        name="prep",
    )(count, bt.reshape(1,NB), bt.reshape(NB,1), bs.reshape(NB,1))

NCH=8
def group_loop(slots, grp, F, buf, sem, body, before):
    for k in range(NCH):
        pltpu.make_async_copy(F.at[pl.ds(k*NB//NCH,NB//NCH)], buf.at[pl.ds(k*NB//NCH,NB//NCH)], sem.at[k]).start()
    before()
    for k in range(NCH):
        pltpu.make_async_copy(F.at[pl.ds(k*NB//NCH,NB//NCH)], buf.at[pl.ds(k*NB//NCH,NB//NCH)], sem.at[k]).wait()
    turns=lax.shift_right_logical(grp[0,127]+(UN-1),2)
    def turn(i,c):
        body(i)
        return c
    lax.fori_loop(0,turns,turn,0)

def rows(slots,buf,g):
    out=[]
    for k in range(4):
        v=slots[0,4*g+k]
        out.append(buf[lax.shift_right_logical(jnp.maximum(v-1,0),6)])
    return jnp.concatenate(out,axis=0)

def snd(slots,g,k):
    v=slots[0,4*g+k]
    return jnp.where(v==0,32,jnp.bitwise_and(v-1,63))

def t_kernel(slots, grp, F, w, pa, pb, acc, wt0, wt1, buf, sem):
    def before():
        lane=lax.broadcasted_iota(jnp.int32,(128,128),1)
        for p in range(16):
            x=jnp.concatenate([w[2*p],w[2*p+1]],axis=0).astype(jnp.float32).T
            y=pltpu.roll(x,64,1)
            lo=lane<64
            z=jnp.zeros_like(x)
            wt0[2*p]=jnp.where(lo,x,z).astype(jnp.bfloat16)
            wt1[2*p]=jnp.where(lo,z,y).astype(jnp.bfloat16)
            wt0[2*p+1]=jnp.where(lo,y,z).astype(jnp.bfloat16)
            wt1[2*p+1]=jnp.where(lo,z,x).astype(jnp.bfloat16)
        wt0[32]=jnp.zeros((128,128),jnp.bfloat16)
        wt1[32]=jnp.zeros((128,128),jnp.bfloat16)
        acc[...]=jnp.zeros_like(acc)
    def body(i):
        outs=[]
        for j in range(UN):
            g=i*UN+j
            s=[snd(slots,g,k) for k in range(4)]
            lhs=jnp.concatenate([wt0[s[0]]+wt1[s[1]],wt0[s[2]]+wt1[s[3]]],axis=1)
            outs.append(jnp.dot(lhs,rows(slots,buf,g),preferred_element_type=jnp.float32))
        for j in range(UN):
            t=grp[0,i*UN+j]
            acc[t]+=outs[j]
    group_loop(slots,grp,F,buf,sem,body,before)
    for y in range(4):
        for z in range(4):
            for c in range(2):
                x=acc[(y*4+z)*2+c].astype(pa.dtype)
                pa[c,y,z]=x[0:64]
                pb[c,z,y]=x[64:128]

SM=pl.BlockSpec(memory_space=pltpu.SMEM); VM=pl.BlockSpec(memory_space=pltpu.VMEM); AN=pl.BlockSpec(memory_space=pl.ANY)
def transpose_map(slots, grp, F, w, dtype):
    o=jax.ShapeDtypeStruct((2,4,4,64,256),dtype)
    return pl.pallas_call(t_kernel,out_shape=(o,o),in_specs=[SM,SM,AN,VM],out_specs=(VM,VM),
        scratch_shapes=[pltpu.VMEM((33,128,256),jnp.float32),pltpu.VMEM((33,128,128),jnp.bfloat16),pltpu.VMEM((33,128,128),jnp.bfloat16),
            pltpu.VMEM((NB,64,256),jnp.bfloat16),pltpu.SemaphoreType.DMA((NCH,))],
        compiler_params=pltpu.CompilerParams(vmem_limit_bytes=32<<20), name="tmap")(slots,grp,F,w)

def f_kernel(slots, grp, F, va, vb, img, acc, buf, sem):
    def before():
        acc[...]=jnp.zeros_like(acc)
    def body(i):
        outs=[]
        for j in range(UN):
            g=i*UN+j
            t=jnp.minimum(grp[0,g],31)
            c=jnp.bitwise_and(t,1); yz=lax.shift_right_logical(t,1)
            zy=jnp.bitwise_and(yz,3)*4+lax.shift_right_logical(yz,2)
            rhs=jnp.concatenate([va[c,yz],vb[c,zy]],axis=0)
            outs.append(jnp.dot(rows(slots,buf,g),rhs,preferred_element_type=jnp.float32))
        for j in range(UN):
            for k in range(4):
                s=snd(slots,i*UN+j,k)
                acc[s]+=outs[j][64*k:64*k+64]
    group_loop(slots,grp,F,buf,sem,body,before)
    img[...]=acc[0:32].astype(img.dtype)

def forward_map(slots, grp, F, va, vb, dtype):
    return pl.pallas_call(f_kernel,out_shape=jax.ShapeDtypeStruct((32,64,128),dtype),in_specs=[SM,SM,AN,VM,VM],out_specs=VM,
        scratch_shapes=[pltpu.VMEM((33,64,128),jnp.float32),pltpu.VMEM((NB,64,256),jnp.bfloat16),pltpu.SemaphoreType.DMA((NCH,))],
        compiler_params=pltpu.CompilerParams(vmem_limit_bytes=32<<20), name="fmap")(slots,grp,F,va.reshape(2,16,128,128),vb.reshape(2,16,128,128))
MESH=pl.DeviceIdType.MESH
f32=jnp.float32; bf16=jnp.bfloat16

class Net:
    def __init__(self, send, recv):
        self.send, self.recv, self.n = send, recv, 0
    def put(self, src, dst, dev):
        k=self.n; self.n+=1
        c=pltpu.make_async_remote_copy(src_ref=src,dst_ref=dst,send_sem=self.send.at[k],recv_sem=self.recv.at[k],device_id=dev,device_id_type=MESH)
        c.start()
        return c

def place():
    o=lax.axis_index("orbit"); r=lax.axis_index("region")
    y=o//8; z=(o//2)%4; c=o%2
    return y,z,c,r
def dev(y,z,c,r): return (y*8+z*2+c, r)

def greet(devs):
    bar=pltpu.get_barrier_semaphore()
    for d in devs:
        pl.semaphore_signal(bar,inc=1,device_id=d,device_id_type=MESH)
    pl.semaphore_wait(bar,len(devs))

class Ring:
    def __init__(self, i, at):
        self.i=i; self.right=(i+1)%4; self.left=(i+3)%4; self.opp=(i+2)%4
        self.dr=at(self.right); self.dl=at(self.left)
        self.b1=at(i+1-2*(i%2)); self.b2=at(3-i)

def rs_begin(net, ring, q, ri, gr, gl):
    h=q.shape[1]//2
    ra=net.put(q.at[ring.opp,pl.ds(0,h)], ri.at[0], ring.dr)
    la=net.put(q.at[ring.opp,pl.ds(h,h)], ri.at[1], ring.dl)
    rb=net.put(q.at[ring.right,pl.ds(h,h)], gr.at[pl.ds(h,h)], ring.dr)
    lb=net.put(q.at[ring.left,pl.ds(0,h)], gl.at[pl.ds(0,h)], ring.dl)
    return [ra,la,rb,lb]
def rs_relay(net, ring, q, ri, so, gr, gl, cs):
    h=q.shape[1]//2
    cs[0].wait_recv()
    so[0]=(q[ring.right,pl.ds(0,h)].astype(f32)+ri[0].astype(f32)).astype(so.dtype)
    cs.append(net.put(so.at[0], gr.at[pl.ds(0,h)], ring.dr))
    cs[1].wait_recv()
    so[1]=(q[ring.left,pl.ds(h,h)].astype(f32)+ri[1].astype(f32)).astype(so.dtype)
    cs.append(net.put(so.at[1], gl.at[pl.ds(h,h)], ring.dl))
def rs_end(cs):
    for c in cs[2:]: c.wait_recv()
def drain(cs):
    for c in cs: c.wait_send()

def ag_begin(net, ring, x):
    s=x.at[ring.i]
    return [net.put(s,s,ring.dr), net.put(s,s,ring.dl)]
def ag_relay(net, ring, x, cs):
    h=x.shape[1]//2
    cs[0].wait_recv()
    s=x.at[ring.left,pl.ds(0,h)]
    cs.append(net.put(s,s,ring.dr))
    cs[1].wait_recv()
    s=x.at[ring.right,pl.ds(h,h)]
    cs.append(net.put(s,s,ring.dl))
def ag_end(cs):
    cs[2].wait_recv(); cs[3].wait_recv()

def hop(net, sin, sout, k, d):
    return net.put(sout.at[k], sin.at[k], d)

def rs_scratch(dt, cdt):
    V=pltpu.VMEM
    out=[V((4,4,64,256),cdt)]*2
    out+=[V((4,4,64,256),dt)]*2
    out+=[V((2,2,64,256),dt),V((2,2,64,256),dt),V((4,64,256),dt),V((4,64,256),dt)]*2
    out+=[V((4,64,256),dt)]*2
    out+=[V((2,32,256),dt),V((2,32,256),dt),V((64,256),dt),V((64,256),dt)]*2
    return out

def reduce_tiles(net, pos, ry, rz, pa, pb, sc, tick=lambda k:None):
    y,z,c,r=pos
    ra,rb,qa,qb=sc[0:4]; a1=sc[4:8]; b1=sc[8:12]; sa,sb=sc[12:14]; a2=sc[14:18]; b2=sc[18:22]
    mate=dev(y,z,1-c,r)
    ks=[]
    oy=[ry.opp,ry.right,ry.left,ry.i]; oz=[rz.opp,rz.right,rz.left,rz.i]
    for k in range(4):
        ks.append((net.put(pa.at[1-c,oy[k]],ra.at[oy[k]],mate), net.put(pb.at[1-c,oz[k]],rb.at[oz[k]],mate)))
    tick(0)
    for k in range(4):
        ks[k][0].wait_recv()
        qa[oy[k]]=(pa[c,oy[k]].astype(f32)+ra[oy[k]].astype(f32)).astype(qa.dtype)
        ks[k][1].wait_recv()
        qb[oz[k]]=(pb[c,oz[k]].astype(f32)+rb[oz[k]].astype(f32)).astype(qb.dtype)
        if k==2:
            ca=rs_begin(net,ry,qa,a1[0],a1[2],a1[3])
            cb=rs_begin(net,rz,qb,b1[0],b1[2],b1[3])
    tick(1)
    rs_relay(net,ry,qa,*a1,ca); rs_relay(net,rz,qb,*b1,cb)
    tick(2)
    rs_end(ca)
    sa[...]=(qa[ry.i].astype(f32)+a1[2][...].astype(f32)+a1[3][...].astype(f32)).astype(sa.dtype)
    da=rs_begin(net,rz,sa,a2[0],a2[2],a2[3])
    rs_end(cb)
    sb[...]=(qb[rz.i].astype(f32)+b1[2][...].astype(f32)+b1[3][...].astype(f32)).astype(sb.dtype)
    db=rs_begin(net,ry,sb,b2[0],b2[2],b2[3])
    tick(3)
    rs_relay(net,rz,sa,*a2,da); rs_relay(net,ry,sb,*b2,db)
    tick(4)
    own_a=qa[ry.i,rz.i].astype(f32)+a1[2][rz.i].astype(f32)+a1[3][rz.i].astype(f32)
    rs_end(da)
    own_a=own_a+a2[2][...].astype(f32)+a2[3][...].astype(f32)
    own_b=qb[rz.i,ry.i].astype(f32)+b1[2][ry.i].astype(f32)+b1[3][ry.i].astype(f32)
    rs_end(db)
    own_b=own_b+b2[2][...].astype(f32)+b2[3][...].astype(f32)
    flat=[x for p in ks for x in p]+ca+cb+da+db
    return jnp.concatenate([own_a,own_b],axis=0), flat

def gather_tiles(net, pos, ry, rz, va, vb, tick=lambda k:None):
    y,z,c,r=pos
    mate=dev(y,z,1-c,r)
    a=ag_begin(net,rz,va.at[c,ry.i]); b=ag_begin(net,ry,vb.at[c,rz.i])
    tick(0)
    ag_relay(net,rz,va.at[c,ry.i],a); ag_relay(net,ry,vb.at[c,rz.i],b)
    tick(1)
    ag_end(a); a2=ag_begin(net,ry,va.at[c])
    ag_end(b); b2=ag_begin(net,rz,vb.at[c])
    ks=[]
    def across(v,i):
        s=v.at[c,i]
        ks.append(net.put(s,s,mate))
    across(va,ry.i); across(vb,rz.i)
    tick(2)
    ag_relay(net,ry,va.at[c],a2); ag_relay(net,rz,vb.at[c],b2)
    across(va,ry.left); across(va,ry.right); across(vb,rz.left); across(vb,rz.right)
    tick(3)
    ag_end(a2); across(va,ry.opp)
    ag_end(b2); across(vb,rz.opp)
    for k in ks: k.wait_recv()
    return a+b+a2+b2+ks

class Reduce:
    def __init__(self, net, sin, sout, hops, base=0):
        self.net, self.sin, self.sout, self.hops, self.base = net, sin, sout, hops, base
        self.k=0; self.cs=[]
    def start(self, value):
        self.value=value
        self._send()
    def _send(self):
        j=self.base+self.k
        self.sout[j]=self.value
        self.cs.append(self.net.put(self.sout.at[j], self.sin.at[j], self.hops[self.k]))
    def step(self):
        j=self.base+self.k
        self.cs[self.k].wait_recv()
        self.value=self.value+self.sin[j]
        self.k+=1
        if self.k<len(self.hops): self._send()
    def finish(self):
        while self.k<len(self.hops): self.step()
        return self.value

def rep(v):
    return jnp.broadcast_to(v,(8,128))
NS=96

def first_kernel(pa, pb, prior, r0, va, vb, npl, *s):
    sc=s[:22]; sin,sout,ssem,rsem=s[22:]
    pos=y,z,c,r=place()
    ry=Ring(y,lambda i:dev(i,z,c,r)); rz=Ring(z,lambda i:dev(y,i,c,r))
    greet([dev(y,z,1-c,r),ry.dr,ry.dl,rz.dr,rz.dl])
    net=Net(ssem,rsem)
    t,cs=reduce_tiles(net,pos,ry,rz,pa,pb,sc)
    res=prior[...]*t.T
    r0[...]=res
    v=(prior[...]*res).astype(bf16)
    va[c,y,z]=v[0:128]; vb[c,z,y]=v[128:256]
    red=Reduce(net,sin,sout,[dev(y,z,1-c,r),ry.b1,ry.b2,rz.b1,rz.b2])
    def tick(k):
        if k==0: red.start(rep(jnp.sum(res*res,axis=0,keepdims=True)))
        else: red.step()
    cs2=gather_tiles(net,pos,ry,rz,va,vb,tick)
    npl[...]=red.finish()
    drain(cs+cs2+red.cs)

def mid_kernel(pa, pb, prior, r0, nrm, wi, r1, d1, it, nn, va, vb, dd, *s):
    sc=s[:22]; sin,sout,ssem,rsem=s[22:]
    pos=y,z,c,r=place()
    ry=Ring(y,lambda i:dev(i,z,c,r)); rz=Ring(z,lambda i:dev(y,i,c,r)); rx=Ring(r,lambda i:dev(y,z,c,i))
    greet([dev(y,z,1-c,r),ry.dr,ry.dl,rz.dr,rz.dl,rx.dr,rx.dl])
    net=Net(ssem,rsem)
    plane=[dev(y,z,1-c,r),ry.b1,ry.b2,rz.b1,rz.b2]
    ra=Reduce(net,sin,sout,plane,0)
    def tick(k):
        if k==0: ra.start(wi[...])
        else: ra.step()
    t,cs=reduce_tiles(net,pos,ry,rz,pa,pb,sc,tick)
    n0=nrm[0:1]
    step=n0/(n0+ra.finish()[0:1])
    d0=r0[...]
    p=d0+prior[...]*t.T
    res=d0-step*p
    rb=Reduce(net,sin,sout,plane+[rx.b1,rx.b2],5)
    rb.start(rep(jnp.sum(res*res,axis=0,keepdims=True)))
    it[...]=step*d0
    r1[...]=res
    n1=rb.finish()
    nn[...]=n1
    d=res+(n1[0:1]/n0)*d0
    d1[...]=d
    v=(prior[...]*d).astype(bf16)
    va[c,y,z]=v[0:128]; vb[c,z,y]=v[128:256]
    rc=Reduce(net,sin,sout,plane,12)
    def tick2(k):
        if k==0: rc.start(rep(jnp.sum(d*d,axis=0,keepdims=True)))
        else: rc.step()
    cs2=gather_tiles(net,pos,ry,rz,va,vb,tick2)
    dd[...]=rc.finish()
    drain(cs+cs2+ra.cs+rb.cs+rc.cs)

def last_kernel(pa, pb, prior, r1, d1, it, n1, dd, wi, flux, resid, *s):
    sc=s[:22]; sin,sout,ssem,rsem=s[22:]
    pos=y,z,c,r=place()
    ry=Ring(y,lambda i:dev(i,z,c,r)); rz=Ring(z,lambda i:dev(y,i,c,r))
    greet([dev(y,z,1-c,r),ry.dr,ry.dl,rz.dr,rz.dl])
    net=Net(ssem,rsem)
    ra=Reduce(net,sin,sout,[dev(y,z,1-c,r),ry.b1,ry.b2,rz.b1,rz.b2],0)
    def tick(k):
        if k==0: ra.start(wi[...])
        else: ra.step()
    t,cs=reduce_tiles(net,pos,ry,rz,pa,pb,sc,tick)
    step=n1[0:1]/(dd[0:1]+ra.finish()[0:1])
    p=d1[...]+prior[...]*t.T
    resid[...]=r1[...]-step*p
    flux[...]=prior[...]*(it[...]+step*d1[...])
    drain(cs+ra.cs)

def cross_kernel(img, wgt, part, w, tot, wi, ri, so, gr, gl, sin, sout, ssem, rsem):
    pos=y,z,c,r=place()
    rx=Ring(r,lambda i:dev(y,z,c,i))
    greet([rx.dr,rx.dl])
    net=Net(ssem,rsem)
    cs=rs_begin(net,rx,img,ri,gr,gl)
    ra=Reduce(net,sin,sout,[rx.b1,rx.b2],0)
    ra.start(part[...])
    rs_relay(net,rx,img,ri,so,gr,gl,cs)
    ra.step()
    rs_end(cs)
    total=img[r].astype(f32)+gr[...].astype(f32)+gl[...].astype(f32)
    wt=wgt[...]
    scaled=wt*total
    w[r]=scaled.astype(bf16)
    ag=ag_begin(net,rx,w)
    rb=Reduce(net,sin,sout,[rx.b1,rx.b2],2)
    rb.start(rep(jnp.sum(jnp.sum(scaled*total,axis=0),axis=0,keepdims=True)))
    ag_relay(net,rx,w,ag)
    rb.step()
    tot[...]=ra.finish()
    wi[...]=rb.finish()
    ag_end(ag)
    drain(cs+ag+ra.cs+rb.cs)

VM=pl.BlockSpec(memory_space=pltpu.VMEM)
def _call(kernel, outs, scratch, cid, name, *args):
    return pl.pallas_call(kernel,out_shape=outs,in_specs=[VM]*len(args),out_specs=tuple([VM]*len(outs)),
        scratch_shapes=scratch,compiler_params=pltpu.CompilerParams(collective_id=cid,has_side_effects=True,vmem_limit_bytes=40<<20),name=name)(*args)
SH=lambda shape,dt=f32: jax.ShapeDtypeStruct(shape,dt)
VA=SH((2,4,4,128,128),bf16); ROW=SH((8,128)); TILE=SH((256,128))
def tail(n): return [pltpu.VMEM((n,8,128),f32)]*2+[pltpu.SemaphoreType.DMA((NS,))]*2
def first(pa,pb,prior):
    return _call(first_kernel,[TILE,VA,VA,ROW],rs_scratch(f32,f32)+tail(5),0,"first",pa,pb,prior)
def mid(pa,pb,prior,r0,nrm,wi):
    return _call(mid_kernel,[TILE,TILE,TILE,ROW,VA,VA,ROW],rs_scratch(bf16,pa.dtype)+tail(17),1,"mid",pa,pb,prior,r0,nrm,wi)
def last(pa,pb,prior,r1,d1,it,n1,dd,wi):
    return _call(last_kernel,[TILE,TILE],rs_scratch(bf16,pa.dtype)+tail(5),2,"last",pa,pb,prior,r1,d1,it,n1,dd,wi)
def cross(img,wgt,part):
    V=pltpu.VMEM
    return _call(cross_kernel,[SH((4,8,64,128),bf16),ROW,ROW],[V((2,4,64,128),bf16)]*2+[V((8,64,128),bf16)]*2+tail(4),3,"cross",img.reshape(4,8,64,128),wgt,part)

def per_device(footprints, block_sounding, block_tile, block_count, observations, obs_weight, prior_std):
    slots, grp = prep(block_count, block_sounding, block_tile)
    w0 = (obs_weight[:, :, None] * observations).astype(bf16)
    prior = jnp.broadcast_to(prior_std.reshape(256, 1), (256, 128))
    mine = lax.dynamic_slice_in_dim(obs_weight, 8 * lax.axis_index("region"), 8, 0)
    wgt = jnp.broadcast_to(mine[:, :, None], (8, 64, 128))
    pa, pb = transpose_map(slots, grp, footprints, w0, f32)
    r0, va, vb, norm = first(pa, pb, prior)
    img = forward_map(slots, grp, footprints, va, vb, bf16)
    w, norm, wi = cross(img, wgt, norm)
    pa, pb = transpose_map(slots, grp, footprints, w.reshape(32, 64, 128), f32)
    r1, d1, it, n1, va, vb, dd = mid(pa, pb, prior, r0, norm, wi)
    img = forward_map(slots, grp, footprints, va, vb, bf16)
    w, dd, wi = cross(img, wgt, dd)
    pa, pb = transpose_map(slots, grp, footprints, w.reshape(32, 64, 128), bf16)
    flux, resid = last(pa, pb, prior, r1, d1, it, n1, dd, wi)
    return flux[None, None], resid[None, None]


def solution(mesh):
    return jax.shard_map(
        per_device,
        mesh=mesh,
        in_specs=(
            P(("orbit", "region"), None, None),
            P(("orbit", "region")),
            P(("orbit", "region")),
            P(("orbit", "region")),
            P("orbit", None, None),
            P("orbit", None),
            P("region", "orbit", None),
        ),
        out_specs=(P("region", "orbit", None, None), P("region", "orbit", None, None)),
        check_vma=False,
    )
```

```python
import jax
import jax.numpy as jnp
from jax import lax
from jax.experimental import pallas as pl
from jax.experimental.pallas import tpu as pltpu
from jax.sharding import PartitionSpec as P

f32 = jnp.float32
bf16 = jnp.bfloat16
def SH(shape, dtype=f32): return jax.ShapeDtypeStruct(shape, dtype)

NB=320; NBP=384; NSLOT=512; UN=16; NCH=4

def sort_blocks(n, bt_row, bt_col, bs_col):
    iota=lambda shape,d: lax.broadcasted_iota(jnp.int32, shape, d)
    trow=jnp.where(iota((1,NBP),1)<n, bt_row, 32.0)
    live=iota((NBP,1),0)<n
    tcol=jnp.where(live, bt_col, 32.0)
    same=(trow==tcol)&(iota((NBP,NBP),1)<iota((NBP,NBP),0))
    rank=jnp.sum(jnp.where(same,1.0,0.0),axis=1,keepdims=True)
    lane=iota((NBP,128),1); lanef=lane.astype(f32)
    num=jnp.sum(jnp.where((tcol==lanef)&(lane<32),1.0,0.0),axis=0,keepdims=True)
    g=jnp.floor((num+3.0)*0.25)
    start=jnp.sum(jnp.where(lanef<tcol,jnp.broadcast_to(g,(NBP,128)),0.0),axis=1,keepdims=True)
    pos=jnp.where(live,4.0*start+rank,-1.0).astype(jnp.int32)
    ident=iota((NBP,1),0).astype(f32)*64.0+bs_col+1.0
    hit=pos==iota((NBP,NSLOT),1)
    slots=jnp.sum(jnp.where(hit,jnp.broadcast_to(ident,(NBP,NSLOT)),0.0),axis=0,keepdims=True)
    l2=iota((128,128),1); s2=iota((128,128),0)
    gend=jnp.sum(jnp.where(l2<=s2,jnp.broadcast_to(g,(128,128)),0.0),axis=1,keepdims=True)
    gt=jnp.sum(jnp.where((s2<32)&(gend<=l2.astype(f32)),1.0,0.0),axis=0,keepdims=True)
    total=jnp.sum(g,axis=1,keepdims=True)
    return slots, jnp.where(iota((1,128),1)==127,jnp.broadcast_to(total,(1,128)),gt)

def begin_kernel(cnt, packed, obs_in, weight_in, prior_in, plan, w0, wgt, pri, obs, weight, prior, sem):
    small=[pltpu.make_async_copy(a,b,sem.at[k]) for k,(a,b) in enumerate(((prior_in,prior),(weight_in,weight),(obs_in,obs)))]
    for c in small: c.start()
    p=packed[...].astype(f32)
    q=p.T
    slots,gt=sort_blocks(cnt[0],p[0:1],q[:,0:1],q[:,1:2])
    plan[0:1]=slots.astype(jnp.int32)
    plan[1:2,0:128]=gt.astype(jnp.int32)
    for c in small: c.wait()
    pri[...]=jnp.broadcast_to(prior[...],(128,256)).T
    own=pl.multiple_of(8*lax.axis_index("region"),8)
    def spread(x): return jnp.broadcast_to(x,(128,64)).T
    mine=weight[pl.ds(own,8)]
    for k in range(8):
        wgt[k]=spread(mine[k:k+1])
    every=weight[...]
    for k in range(32):
        w0[k]=(spread(every[k:k+1])*obs[k]).astype(bf16)

SM=pl.BlockSpec(memory_space=pltpu.SMEM); VM=pl.BlockSpec(memory_space=pltpu.VMEM); HB=pl.BlockSpec(memory_space=pltpu.MemorySpace.HBM)
def begin(cnt, bs, bt, obs, weight, prior):
    packed=jnp.pad(jnp.stack([bt,bs]),((0,6),(0,NBP-NB)))
    return pl.pallas_call(begin_kernel,
        out_shape=(SH((2,NSLOT),jnp.int32),SH((32,64,128),bf16),SH((8,64,128)),SH((256,128))),
        in_specs=[SM,VM,HB,HB,HB],out_specs=(VM,)*4,
        scratch_shapes=[pltpu.VMEM((32,64,128),f32),pltpu.VMEM((32,64),f32),pltpu.VMEM((1,256),f32),pltpu.SemaphoreType.DMA((3,))],
        cost_estimate=pl.CostEstimate(flops=10**10,bytes_accessed=3*10**7,transcendentals=0),
        compiler_params=pltpu.CompilerParams(vmem_limit_bytes=10<<20),name="begin")(cnt,packed,obs,weight,prior)

def snd(plan,g,k):
    v=plan[0,4*g+k]
    return jnp.where(v==0,32,jnp.bitwise_and(v-1,63))
def group_loop(plan, body):
    turns=(plan[1,127]+(UN-1))//UN
    def turn(i,c):
        body(i)
        return c
    lax.fori_loop(0,turns,turn,0)
def four(plan,F,g):
    out=[]
    for k in range(4):
        v=plan[0,4*g+k]
        out.append(F[lax.shift_right_logical(jnp.maximum(v-1,0),6)])
    return jnp.concatenate(out,axis=0)

def t_kernel(plan, F, w, pa, pb, acc, wt0, wt1):
    lane=lax.broadcasted_iota(jnp.int32,(128,128),1)
    for p in range(16):
        x=jnp.concatenate([w[2*p],w[2*p+1]],axis=0).astype(f32).T
        y=pltpu.roll(x,64,1)
        lo=lane<64
        z=jnp.zeros_like(x)
        wt0[2*p]=jnp.where(lo,x,z).astype(bf16)
        wt1[2*p]=jnp.where(lo,z,y).astype(bf16)
        wt0[2*p+1]=jnp.where(lo,y,z).astype(bf16)
        wt1[2*p+1]=jnp.where(lo,z,x).astype(bf16)
    wt0[32]=jnp.zeros((128,128),bf16)
    wt1[32]=jnp.zeros((128,128),bf16)
    acc[...]=jnp.zeros_like(acc)
    def body(i):
        for j in range(UN):
            g=i*UN+j
            s=[snd(plan,g,k) for k in range(4)]
            lhs=jnp.concatenate([wt0[s[0]]+wt1[s[1]],wt0[s[2]]+wt1[s[3]]],axis=1)
            acc[plan[1,g]]+=jnp.dot(lhs,four(plan,F,g),preferred_element_type=f32)
    group_loop(plan,body)
    for y in range(4):
        for z in range(4):
            for c in range(2):
                x=acc[(y*4+z)*2+c].astype(pa.dtype)
                pa[c,z,y]=x[0:64]
                pb[c,y,z]=x[64:128]
def transpose_map(plan, F, w, dtype):
    o=SH((2,4,4,64,256),dtype)
    return pl.pallas_call(t_kernel,out_shape=(o,o),in_specs=[SM,VM,VM],out_specs=(VM,VM),
        scratch_shapes=[pltpu.VMEM((33,128,256),f32),pltpu.VMEM((33,128,128),bf16),pltpu.VMEM((33,128,128),bf16)],
        compiler_params=pltpu.CompilerParams(vmem_limit_bytes=24<<20), name="tmap")(plan,F,w)

def f_kernel(plan, F, va, vb, img, acc):
    acc[...]=jnp.zeros_like(acc)
    def body(i):
        for j in range(UN):
            g=i*UN+j
            t=jnp.minimum(plan[1,g],31)
            c=jnp.bitwise_and(t,1); z=jnp.bitwise_and(lax.shift_right_logical(t,1),3); y=lax.shift_right_logical(t,3)
            rhs=jnp.concatenate([va[c,z*4+y],vb[c,y*4+z]],axis=0)
            out=jnp.dot(four(plan,F,g),rhs,preferred_element_type=f32)
            for k in range(4):
                acc[snd(plan,g,k)]+=out[64*k:64*k+64]
    group_loop(plan,body)
    img[...]=acc[0:32].astype(img.dtype)
def forward_map(plan, F, va, vb):
    return pl.pallas_call(f_kernel,out_shape=SH((32,64,128),bf16),in_specs=[SM,VM,VM,VM],out_specs=VM,
        scratch_shapes=[pltpu.VMEM((33,64,128),f32)],
        compiler_params=pltpu.CompilerParams(vmem_limit_bytes=18<<20), name="fmap")(plan,F,va.reshape(2,16,128,128),vb.reshape(2,16,128,128))

MESH=pl.DeviceIdType.MESH
class Net:
    def __init__(self, send, recv):
        self.send, self.recv, self.ns, self.nr, self.owed = send, recv, 0, 0, []
    def sender(self, whole):
        k=self.ns; self.ns+=1
        self.owed.append((k,whole))
        return k
    def taker(self):
        k=self.nr; self.nr+=1
        return k
    def put(self, src, dst, dev, sk, rk):
        pltpu.make_async_remote_copy(src_ref=src,dst_ref=dst,send_sem=self.send.at[sk],recv_sem=self.recv.at[rk],device_id=dev,device_id_type=MESH).start()
    def take(self, rk, whole):
        pltpu.make_async_copy(whole,whole,self.recv.at[rk]).wait()
    def drain(self):
        for k,whole in self.owed:
            pltpu.make_async_copy(whole,whole,self.send.at[k]).wait()

def place():
    o=lax.axis_index("orbit"); r=lax.axis_index("region")
    return o//8,(o//2)%4,o%2,r
def dev(y,z,c,r): return (y*8+z*2+c, r)
def greet(devs):
    bar=pltpu.get_barrier_semaphore()
    for d in devs:
        pl.semaphore_signal(bar,inc=1,device_id=d,device_id_type=MESH)
    pl.semaphore_wait(bar,len(devs))

class Ring:
    def __init__(self, i, at):
        self.i=i
        self.to=[(i+d)%4 for d in range(4)]
        self.dev=[at((i+d)%4) for d in range(4)]
    def peers(self): return self.dev[1:4]
FAR=(2,1,3)

def reduce_scratch(dt, cdt):
    V=pltpu.VMEM
    return [V((4,4,64,256),cdt)]*2+[V((4,4,64,256),dt)]*2+[V((3,4,64,256),dt)]*2+[V((3,64,256),dt)]*4

def reduce_tiles(net, mate, c, ry, rz, pa, pb, sc, tick=lambda k:None):
    ra,rb,qa,qb,ga,gb,sa,sb,ha,hb=sc
    sides=((ry,rz,pa,ra,qa,ga,sa,ha),(rz,ry,pb,rb,qb,gb,sb,hb))
    order=(2,1,3,0)
    s0=[net.sender(r) for (m,n,p,r,q,g,s,h) in sides]
    k0=[[net.taker() for x in sides] for e in order]
    for k,e in enumerate(order):
        for b,(m,n,p,r,q,g,s,h) in enumerate(sides):
            net.put(p.at[1-c,n.to[e]],r.at[n.to[e]],mate,s0[b],k0[k][b])
    tick(0)
    s1=[net.sender(g) for (m,n,p,r,q,g,s,h) in sides]
    k1=[[net.taker() for x in sides] for e in order]
    for k,e in enumerate(order):
        for b,(m,n,p,r,q,g,s,h) in enumerate(sides):
            j=n.to[e]
            net.take(k0[k][b],r.at[j])
            for d in FAR:
                q[j,m.to[d]]=(p[c,j,m.to[d]].astype(f32)+r[j,m.to[d]].astype(f32)).astype(q.dtype)
                net.put(q.at[j,m.to[d]],g.at[d-1,j],m.dev[d],s1[b],k1[k][b])
    tick(1)
    s2=[net.sender(s) for (m,n,p,r,q,g,s,h) in sides]
    k2=[net.taker() for x in sides]
    own=[None,None]
    for k,e in enumerate(order):
        for b,(m,n,p,r,q,g,s,h) in enumerate(sides):
            j=n.to[e]
            x=p[c,j,m.i].astype(f32)+r[j,m.i].astype(f32)
            net.take(k1[k][b],h)
            x=x+(g[0,j].astype(f32)+g[1,j].astype(f32)+g[2,j].astype(f32))
            if e:
                s[e-1]=x.astype(s.dtype)
                net.put(s.at[e-1],h.at[e-1],n.dev[e],s2[b],k2[b])
            else: own[b]=x
    tick(2)
    for b,(m,n,p,r,q,g,s,h) in enumerate(sides):
        net.take(k2[b],h)
        own[b]=own[b]+(h[0].astype(f32)+h[1].astype(f32)+h[2].astype(f32))
    return jnp.concatenate(own,axis=0)

def gather_tiles(net, mate, c, ry, rz, va, vb, tick=lambda k:None):
    sides=((ry,rz,va),(rz,ry,vb))
    three=[v.at[0,0,pl.ds(0,3)] for m,n,v in sides]
    s1=[net.sender(x) for x in three]
    k1=[[net.taker() for d in range(3)] for x in sides]
    for b,(m,n,v) in enumerate(sides):
        s=v.at[c,n.i,m.i]
        for d in (1,3,2): net.put(s,s,n.dev[d],s1[b],k1[b][d-1])
    tick(0)
    s2=[net.sender(v.at[0,pl.ds(0,3)]) for m,n,v in sides]
    order=(0,3,1,2)
    k2=[[net.taker() for x in sides] for e in order]
    for k,e in enumerate(order):
        for b,(m,n,v) in enumerate(sides):
            s=v.at[c,n.to[e],m.i]
            if e: net.take(k1[b][3-e],s)
            for d in FAR: net.put(s,s,m.dev[d],s2[b],k2[k][b])
    tick(1)
    s3=[net.sender(v.at[0]) for m,n,v in sides]
    k3=[net.taker() for x in sides]
    for k,e in enumerate(order):
        for b,(m,n,v) in enumerate(sides):
            net.take(k2[k][b],three[b])
            s=v.at[c,n.to[e]]
            net.put(s,s,mate,s3[b],k3[b])
        if k==1: tick(2)
    tick(3)
    for b,(m,n,v) in enumerate(sides): net.take(k3[b],v.at[0])

class Reduce:
    def __init__(self, net, sin, sout, axes, base=0):
        self.net, self.sin, self.sout, self.axes = net, sin, sout, axes
        self.at=base; self.so=base; self.k=0
    def start(self, value):
        self.value=value
        self._send()
    def _send(self):
        a=self.axes[self.k]
        self.sout[self.so]=self.value
        sk=self.net.sender(self.sin.at[pl.ds(self.at,len(a))]); self.rk=self.net.taker()
        for i,d in enumerate(a): self.net.put(self.sout.at[self.so],self.sin.at[self.at+i],d,sk,self.rk)
    def step(self):
        n=len(self.axes[self.k])
        self.net.take(self.rk,self.sin.at[pl.ds(self.at,n)])
        for i in range(n): self.value=self.value+self.sin[self.at+i]
        self.at+=n; self.so+=1; self.k+=1
        if self.k<len(self.axes): self._send()
    def finish(self):
        while self.k<len(self.axes): self.step()
        return self.value
def rep(v): return jnp.broadcast_to(v,(8,128))

def first_kernel(pa, pb, prior, r0, va, vb, npl, *s):
    sc=s[:-4]; sin,sout,ssem,rsem=s[-4:]
    y,z,c,r=place(); mate=dev(y,z,1-c,r)
    ry=Ring(y,lambda i:dev(i,z,c,r)); rz=Ring(z,lambda i:dev(y,i,c,r))
    greet([mate]+ry.peers()+rz.peers())
    net=Net(ssem,rsem)
    t=reduce_tiles(net,mate,c,ry,rz,pa,pb,sc)
    res=prior[...]*t.T
    v=(prior[...]*res).astype(bf16)
    va[c,z,y]=v[0:128]; vb[c,y,z]=v[128:256]
    red=Reduce(net,sin,sout,[ry.peers(),rz.peers(),[mate]])
    def tick(k):
        if k==0:
            r0[...]=res
            red.start(rep(jnp.sum(res*res,axis=0,keepdims=True)))
        elif k>1: red.step()
    gather_tiles(net,mate,c,ry,rz,va,vb,tick)
    npl[...]=red.finish()
    net.drain()
    assert (net.ns,net.nr)==FIRST_NET, (net.ns,net.nr)

def mid_kernel(pa, pb, prior, r0, nrm, wi, r1, d1, it, nn, va, vb, dd, *s):
    sc=s[:-4]; sin,sout,ssem,rsem=s[-4:]
    y,z,c,r=place(); mate=dev(y,z,1-c,r)
    ry=Ring(y,lambda i:dev(i,z,c,r)); rz=Ring(z,lambda i:dev(y,i,c,r)); rx=Ring(r,lambda i:dev(y,z,c,i))
    greet([mate]+ry.peers()+rz.peers()+rx.peers())
    net=Net(ssem,rsem)
    plane=[ry.peers(),rz.peers(),[mate]]
    ra=Reduce(net,sin,sout,plane,0)
    def tick(k):
        if k==0: ra.start(wi[...])
        else: ra.step()
    t=reduce_tiles(net,mate,c,ry,rz,pa,pb,sc,tick)
    n0=nrm[0:1]
    step=n0/(n0+ra.finish()[0:1])
    d0=r0[...]
    res=d0-step*(d0+prior[...]*t.T)
    rb=Reduce(net,sin,sout,[[mate],rx.peers(),ry.peers(),rz.peers()],7)
    rb.start(rep(jnp.sum(res*res,axis=0,keepdims=True)))
    it[...]=step*d0
    r1[...]=res
    n1=rb.finish()
    nn[...]=n1
    d=res+(n1[0:1]/n0)*d0
    v=(prior[...]*d).astype(bf16)
    va[c,z,y]=v[0:128]; vb[c,y,z]=v[128:256]
    rc=Reduce(net,sin,sout,plane,17)
    def tick2(k):
        if k==0:
            d1[...]=d
            rc.start(rep(jnp.sum(d*d,axis=0,keepdims=True)))
        elif k>1: rc.step()
    gather_tiles(net,mate,c,ry,rz,va,vb,tick2)
    dd[...]=rc.finish()
    net.drain()
    assert (net.ns,net.nr)==MID_NET, (net.ns,net.nr)

def last_kernel(pa, pb, prior, r1, d1, it, n1, dd, wi, flux, resid, *s):
    sc=s[:-4]; sin,sout,ssem,rsem=s[-4:]
    y,z,c,r=place(); mate=dev(y,z,1-c,r)
    ry=Ring(y,lambda i:dev(i,z,c,r)); rz=Ring(z,lambda i:dev(y,i,c,r))
    greet([mate]+ry.peers()+rz.peers())
    net=Net(ssem,rsem)
    ra=Reduce(net,sin,sout,[ry.peers(),rz.peers(),[mate]],0)
    def tick(k):
        if k==0: ra.start(wi[...])
        else: ra.step()
    t=reduce_tiles(net,mate,c,ry,rz,pa,pb,sc,tick)
    step=n1[0:1]/(dd[0:1]+ra.finish()[0:1])
    p=d1[...]+prior[...]*t.T
    resid[...]=r1[...]-step*p
    flux[...]=prior[...]*(it[...]+step*d1[...])
    net.drain()
    assert (net.ns,net.nr)==LAST_NET, (net.ns,net.nr)

CH=4
def cross_kernel(img, wgt, part, w, tot, wi, g, ri, so, sin, sout, ssem, rsem):
    y,z,c,r=place()
    rx=Ring(r,lambda i:dev(y,z,c,i))
    greet(rx.peers())
    net=Net(ssem,rsem)
    n=8//CH
    B=[pl.ds(j*n,n) for j in range(CH)]
    way=lambda j: 1 if j%2==0 else 3
    sf,sn,sv=net.sender(ri),net.sender(ri),net.sender(ri)
    kf=[net.taker() for j in range(CH)]; kn=[net.taker() for j in range(CH)]
    for j in range(CH): net.put(img.at[rx.to[2],B[j]],ri.at[j],rx.dev[way(j)],sf,kf[j])
    for j in range(CH): net.put(img.at[rx.to[4-way(j)],B[j]],g.at[1 if way(j)==1 else 0,B[j]],rx.dev[4-way(j)],sn,kn[j])
    ra=Reduce(net,sin,sout,[rx.peers()],0)
    ra.start(part[...])
    for j in range(CH):
        net.take(kf[j],ri.at[j])
        so[j]=(img[rx.to[way(j)],B[j]].astype(f32)+ri[j].astype(f32)).astype(bf16)
        net.put(so.at[j],g.at[0 if way(j)==1 else 1,B[j]],rx.dev[way(j)],sv,kn[j])
    sums=jnp.zeros((64,128),f32)
    sa,sr=net.sender(w.at[pl.ds(0,2)]),net.sender(w.at[0])
    ka=[net.taker() for j in range(CH)]; kr=net.taker()
    for j in range(CH):
        b=B[j]
        net.take(kn[j],g.at[0,pl.ds(0,2*n)])
        x=img[r,b].astype(f32)+(g[0,b].astype(f32)+g[1,b].astype(f32))
        m=wgt[b]*x
        w[r,b]=m.astype(bf16)
        s=w.at[r,b]
        net.put(s,s,rx.dev[way(j)],sa,ka[j])
        net.put(s,s,rx.dev[4-way(j)],sa,kr)
        sums=sums+jnp.sum(m*x,axis=0)
    rb=Reduce(net,sin,sout,[rx.peers()],3)
    rb.start(rep(jnp.sum(sums,axis=0,keepdims=True)))
    for j in range(CH):
        s=w.at[rx.to[4-way(j)],B[j]]
        net.take(ka[j],s)
        net.put(s,s,rx.dev[way(j)],sr,kr)
    tot[...]=ra.finish()
    wi[...]=rb.finish()
    net.take(kr,w.at[pl.ds(0,2)])
    net.drain()
    assert (net.ns,net.nr)==CROSS_NET, (net.ns,net.nr)

FIRST_NET=(15,37); MID_NET=(22,44); LAST_NET=(9,21); CROSS_NET=(7,15)
def _call(kernel, outs, scratch, cid, lim, name, *args):
    return pl.pallas_call(kernel,out_shape=outs,in_specs=[VM]*len(args),out_specs=tuple([VM]*len(outs)),
        scratch_shapes=scratch,compiler_params=pltpu.CompilerParams(collective_id=cid,has_side_effects=True,vmem_limit_bytes=lim<<20),name=name)(*args)
VA=SH((2,4,4,128,128),bf16); ROW=SH((8,128)); TILE=SH((256,128))
def tail(n, net): return [pltpu.VMEM((n,8,128),f32)]*2+[pltpu.SemaphoreType.DMA((k,)) for k in net]
def first(pa,pb,prior):
    return _call(first_kernel,[TILE,VA,VA,ROW],reduce_scratch(f32,f32)+tail(7,FIRST_NET),0,22,"first",pa,pb,prior)
def mid(pa,pb,prior,r0,nrm,wi):
    return _call(mid_kernel,[TILE,TILE,TILE,ROW,VA,VA,ROW],reduce_scratch(bf16,pa.dtype)+tail(24,MID_NET),1,18,"mid",pa,pb,prior,r0,nrm,wi)
def last(pa,pb,prior,r1,d1,it,n1,dd,wi):
    return _call(last_kernel,[TILE,TILE],reduce_scratch(bf16,pa.dtype)+tail(7,LAST_NET),2,14,"last",pa,pb,prior,r1,d1,it,n1,dd,wi)
def cross(img,wgt,part):
    return _call(cross_kernel,[SH((4,8,64,128),bf16),ROW,ROW],[pltpu.VMEM((2,8,64,128),bf16),pltpu.VMEM((CH,8//CH,64,128),bf16),pltpu.VMEM((CH,8//CH,64,128),bf16)]+tail(6,CROSS_NET),3,8,"cross",img.reshape(4,8,64,128),wgt,part)

def per_device(footprints, block_sounding, block_tile, block_count, observations, obs_weight, prior_std):
    F = footprints
    plan, w0, wgt, prior = begin(block_count, block_sounding, block_tile, observations, obs_weight, prior_std.reshape(1, 256))
    pa, pb = transpose_map(plan, F, w0, f32)
    r0, va, vb, norm = first(pa, pb, prior)
    img = forward_map(plan, F, va, vb)
    w, norm, wi = cross(img, wgt, norm)
    pa, pb = transpose_map(plan, F, w.reshape(32, 64, 128), f32)
    r1, d1, it, n1, va, vb, dd = mid(pa, pb, prior, r0, norm, wi)
    img = forward_map(plan, F, va, vb)
    w, dd, wi = cross(img, wgt, dd)
    pa, pb = transpose_map(plan, F, w.reshape(32, 64, 128), bf16)
    flux, resid = last(pa, pb, prior, r1, d1, it, n1, dd, wi)
    return flux[None, None], resid[None, None]


def solution(mesh):
    return jax.shard_map(
        per_device,
        mesh=mesh,
        in_specs=(
            P(("orbit", "region"), None, None),
            P(("orbit", "region")),
            P(("orbit", "region")),
            P(("orbit", "region")),
            P("orbit", None, None),
            P("orbit", None),
            P("region", "orbit", None),
        ),
        out_specs=(P("region", "orbit", None, None), P("region", "orbit", None, None)),
        check_vma=False,
    )
```

```python
import jax
import jax.numpy as jnp
from jax import lax
from jax.experimental import pallas as pl
from jax.experimental.pallas import tpu as pltpu
from jax.sharding import PartitionSpec as P

f32 = jnp.float32
bf16 = jnp.bfloat16
def SH(shape, dtype=f32): return jax.ShapeDtypeStruct(shape, dtype)

NB=320; NBP=384; NSLOT=512; UN=24; NCH=4

def sort_blocks(n, bt_row, bt_col, bs_col):
    iota=lambda shape,d: lax.broadcasted_iota(jnp.int32, shape, d)
    trow=jnp.where(iota((1,NBP),1)<n, bt_row, 32.0)
    live=iota((NBP,1),0)<n
    tcol=jnp.where(live, bt_col, 32.0)
    same=(trow==tcol)&(iota((NBP,NBP),1)<iota((NBP,NBP),0))
    rank=jnp.sum(jnp.where(same,1.0,0.0),axis=1,keepdims=True)
    lane=iota((NBP,128),1); lanef=lane.astype(f32)
    num=jnp.sum(jnp.where((tcol==lanef)&(lane<32),1.0,0.0),axis=0,keepdims=True)
    g=jnp.floor((num+3.0)*0.25)
    start=jnp.sum(jnp.where(lanef<tcol,jnp.broadcast_to(g,(NBP,128)),0.0),axis=1,keepdims=True)
    pos=jnp.where(live,4.0*start+rank,-1.0).astype(jnp.int32)
    ident=iota((NBP,1),0).astype(f32)*64.0+bs_col+1.0
    hit=pos==iota((NBP,NSLOT),1)
    slots=jnp.sum(jnp.where(hit,jnp.broadcast_to(ident,(NBP,NSLOT)),0.0),axis=0,keepdims=True)
    l2=iota((128,128),1); s2=iota((128,128),0)
    gend=jnp.sum(jnp.where(l2<=s2,jnp.broadcast_to(g,(128,128)),0.0),axis=1,keepdims=True)
    gt=jnp.sum(jnp.where((s2<32)&(gend<=l2.astype(f32)),1.0,0.0),axis=0,keepdims=True)
    total=jnp.sum(g,axis=1,keepdims=True)
    return slots, jnp.where(iota((1,128),1)==127,jnp.broadcast_to(total,(1,128)),gt)

def sort_kernel(cnt, packed, plan):
    p=packed[...].astype(f32)
    q=p.T
    slots,gt=sort_blocks(cnt[0],p[0:1],q[:,0:1],q[:,1:2])
    plan[0:1]=slots.astype(jnp.int32)
    plan[1:2,0:128]=gt.astype(jnp.int32)

def spread_kernel(obs, weight, prior, w0, wgt, pri):
    pri[...]=jnp.broadcast_to(prior[...],(128,256)).T
    own=pl.multiple_of(8*lax.axis_index("region"),8)
    def spread(x): return jnp.broadcast_to(x,(128,64)).T
    mine=weight[pl.ds(own,8)]
    for k in range(8):
        wgt[k]=spread(mine[k:k+1])
    every=weight[...]
    for k in range(32):
        w0[k]=(spread(every[k:k+1])*obs[k]).astype(bf16)

SM=pl.BlockSpec(memory_space=pltpu.SMEM); VM=pl.BlockSpec(memory_space=pltpu.VMEM)
def begin(cnt, bs, bt, obs, weight, prior):
    packed=jnp.pad(jnp.stack([bt,bs]),((0,6),(0,NBP-NB)))
    plan=pl.pallas_call(sort_kernel,out_shape=SH((2,NSLOT),jnp.int32),in_specs=[SM,VM],out_specs=VM,
        cost_estimate=pl.CostEstimate(flops=10**10,bytes_accessed=3*10**7,transcendentals=0),
        compiler_params=pltpu.CompilerParams(vmem_limit_bytes=8<<20),name="sort")(cnt,packed)
    w0,wgt,pri=pl.pallas_call(spread_kernel,out_shape=(SH((32,64,128),bf16),SH((8,64,128)),SH((256,128))),
        in_specs=[VM]*3,out_specs=(VM,)*3,
        cost_estimate=pl.CostEstimate(flops=10**9,bytes_accessed=4*10**6,transcendentals=0),
        compiler_params=pltpu.CompilerParams(vmem_limit_bytes=8<<20),name="spread")(obs,weight,prior)
    return plan,w0,wgt,pri

def snd(plan,g,k):
    v=plan[0,4*g+k]
    return jnp.where(v==0,32,jnp.bitwise_and(v-1,63))
def group_loop(plan, body):
    turns=(plan[1,127]+(UN-1))//UN
    def turn(i,c):
        body(i)
        return c
    lax.fori_loop(0,turns,turn,0)
def four(plan,F,g):
    out=[]
    for k in range(4):
        v=plan[0,4*g+k]
        out.append(F[lax.shift_right_logical(jnp.maximum(v-1,0),6)])
    return jnp.concatenate(out,axis=0)

def t_kernel(plan, F, w, pa, pb, acc, wt0, wt1):
    lane=lax.broadcasted_iota(jnp.int32,(128,128),1)
    for p in range(16):
        x=jnp.concatenate([w[2*p],w[2*p+1]],axis=0).astype(f32).T
        y=pltpu.roll(x,64,1)
        lo=lane<64
        z=jnp.zeros_like(x)
        wt0[2*p]=jnp.where(lo,x,z).astype(bf16)
        wt1[2*p]=jnp.where(lo,z,y).astype(bf16)
        wt0[2*p+1]=jnp.where(lo,y,z).astype(bf16)
        wt1[2*p+1]=jnp.where(lo,z,x).astype(bf16)
    wt0[32]=jnp.zeros((128,128),bf16)
    wt1[32]=jnp.zeros((128,128),bf16)
    acc[...]=jnp.zeros_like(acc)
    def body(i):
        for j in range(UN):
            g=i*UN+j
            s=[snd(plan,g,k) for k in range(4)]
            lhs=jnp.concatenate([wt0[s[0]]+wt1[s[1]],wt0[s[2]]+wt1[s[3]]],axis=1)
            acc[plan[1,g]]+=jnp.dot(lhs,four(plan,F,g),preferred_element_type=f32)
    group_loop(plan,body)
    for y in range(4):
        for z in range(4):
            for c in range(2):
                x=acc[(y*4+z)*2+c].astype(pa.dtype)
                pa[c,z,y]=x[0:64]
                pb[c,y,z]=x[64:128]
def transpose_map(plan, F, w, dtype):
    o=SH((2,4,4,64,256),dtype)
    return pl.pallas_call(t_kernel,out_shape=(o,o),in_specs=[SM,VM,VM],out_specs=(VM,VM),
        scratch_shapes=[pltpu.VMEM((33,128,256),f32),pltpu.VMEM((33,128,128),bf16),pltpu.VMEM((33,128,128),bf16)],
        compiler_params=pltpu.CompilerParams(vmem_limit_bytes=24<<20), name="tmap")(plan,F,w)

def f_kernel(plan, F, va, vb, img, acc):
    acc[...]=jnp.zeros_like(acc)
    def body(i):
        for j in range(UN):
            g=i*UN+j
            t=jnp.minimum(plan[1,g],31)
            c=jnp.bitwise_and(t,1); z=jnp.bitwise_and(lax.shift_right_logical(t,1),3); y=lax.shift_right_logical(t,3)
            rhs=jnp.concatenate([va[c,z*4+y],vb[c,y*4+z]],axis=0)
            out=jnp.dot(four(plan,F,g),rhs,preferred_element_type=f32)
            for k in range(4):
                acc[snd(plan,g,k)]+=out[64*k:64*k+64]
    group_loop(plan,body)
    img[...]=acc[0:32].astype(img.dtype)
def forward_map(plan, F, va, vb):
    return pl.pallas_call(f_kernel,out_shape=SH((32,64,128),bf16),in_specs=[SM,VM,VM,VM],out_specs=VM,
        scratch_shapes=[pltpu.VMEM((33,64,128),f32)],
        compiler_params=pltpu.CompilerParams(vmem_limit_bytes=18<<20), name="fmap")(plan,F,va.reshape(2,16,128,128),vb.reshape(2,16,128,128))

MESH=pl.DeviceIdType.MESH
class Net:
    def __init__(self, send, recv):
        self.send, self.recv, self.ns, self.nr, self.owed = send, recv, 0, 0, []
    def sender(self, whole):
        k=self.ns; self.ns+=1
        self.owed.append((k,whole))
        return k
    def taker(self):
        k=self.nr; self.nr+=1
        return k
    def put(self, src, dst, dev, sk, rk):
        pltpu.make_async_remote_copy(src_ref=src,dst_ref=dst,send_sem=self.send.at[sk],recv_sem=self.recv.at[rk],device_id=dev,device_id_type=MESH).start()
    def take(self, rk, whole):
        pltpu.make_async_copy(whole,whole,self.recv.at[rk]).wait()
    def drain(self):
        for k,whole in self.owed:
            pltpu.make_async_copy(whole,whole,self.send.at[k]).wait()

def place():
    o=lax.axis_index("orbit"); r=lax.axis_index("region")
    return o//8,(o//2)%4,o%2,r
def dev(y,z,c,r): return (y*8+z*2+c, r)
def greet(devs):
    bar=pltpu.get_barrier_semaphore()
    for d in devs:
        pl.semaphore_signal(bar,inc=1,device_id=d,device_id_type=MESH)
    pl.semaphore_wait(bar,len(devs))

class Ring:
    def __init__(self, i, at):
        self.i=i
        self.to=[(i+d)%4 for d in range(4)]
        self.dev=[at((i+d)%4) for d in range(4)]
    def peers(self): return self.dev[1:4]
FAR=(1,3,2)

def reduce_scratch(dt, cdt):
    V=pltpu.VMEM
    return [V((4,4,64,256),cdt)]*2+[V((4,4,64,256),dt)]*2+[V((3,4,64,256),dt)]*2+[V((3,64,256),dt)]*4

def reduce_tiles(net, mate, c, ry, rz, pa, pb, sc, tick=lambda k:None):
    ra,rb,qa,qb,ga,gb,sa,sb,ha,hb=sc
    sides=((ry,rz,pa,ra,qa,ga,sa,ha),(rz,ry,pb,rb,qb,gb,sb,hb))
    order=(2,1,3,0)
    s0=[net.sender(r) for (m,n,p,r,q,g,s,h) in sides]
    k0=[[net.taker() for x in sides] for e in order]
    for k,e in enumerate(order):
        for b,(m,n,p,r,q,g,s,h) in enumerate(sides):
            net.put(p.at[1-c,n.to[e]],r.at[n.to[e]],mate,s0[b],k0[k][b])
    tick(0)
    s1=[net.sender(g) for (m,n,p,r,q,g,s,h) in sides]
    k1=[[net.taker() for x in sides] for e in order]
    for k,e in enumerate(order):
        for b,(m,n,p,r,q,g,s,h) in enumerate(sides):
            j=n.to[e]
            net.take(k0[k][b],r.at[j])
            for d in FAR:
                q[j,m.to[d]]=(p[c,j,m.to[d]].astype(f32)+r[j,m.to[d]].astype(f32)).astype(q.dtype)
                net.put(q.at[j,m.to[d]],g.at[d-1,j],m.dev[d],s1[b],k1[k][b])
    tick(1)
    s2=[net.sender(s) for (m,n,p,r,q,g,s,h) in sides]
    k2=[net.taker() for x in sides]
    own=[None,None]
    for k,e in enumerate(order):
        for b,(m,n,p,r,q,g,s,h) in enumerate(sides):
            j=n.to[e]
            x=p[c,j,m.i].astype(f32)+r[j,m.i].astype(f32)
            net.take(k1[k][b],h)
            x=x+(g[0,j].astype(f32)+g[1,j].astype(f32)+g[2,j].astype(f32))
            if e:
                s[e-1]=x.astype(s.dtype)
                net.put(s.at[e-1],h.at[e-1],n.dev[e],s2[b],k2[b])
            else: own[b]=x
    tick(2)
    for b,(m,n,p,r,q,g,s,h) in enumerate(sides):
        net.take(k2[b],h)
        own[b]=own[b]+(h[0].astype(f32)+h[1].astype(f32)+h[2].astype(f32))
    return jnp.concatenate(own,axis=0)

def gather_tiles(net, mate, c, ry, rz, va, vb, tick=lambda k:None):
    sides=((ry,rz,va),(rz,ry,vb))
    three=[v.at[0,0,pl.ds(0,3)] for m,n,v in sides]
    s1=[net.sender(x) for x in three]
    k1=[[net.taker() for d in range(3)] for x in sides]
    for b,(m,n,v) in enumerate(sides):
        s=v.at[c,n.i,m.i]
        for d in (1,3,2): net.put(s,s,n.dev[d],s1[b],k1[b][d-1])
    tick(0)
    s2=[net.sender(v.at[0,pl.ds(0,3)]) for m,n,v in sides]
    order=(0,3,1,2)
    k2=[[net.taker() for x in sides] for e in order]
    for k,e in enumerate(order):
        for b,(m,n,v) in enumerate(sides):
            s=v.at[c,n.to[e],m.i]
            if e: net.take(k1[b][3-e],s)
            for d in FAR: net.put(s,s,m.dev[d],s2[b],k2[k][b])
    tick(1)
    s3=[net.sender(v.at[0]) for m,n,v in sides]
    k3=[net.taker() for x in sides]
    for k,e in enumerate(order):
        for b,(m,n,v) in enumerate(sides):
            net.take(k2[k][b],three[b])
            s=v.at[c,n.to[e]]
            net.put(s,s,mate,s3[b],k3[b])
        if k==1: tick(2)
    tick(3)
    for b,(m,n,v) in enumerate(sides): net.take(k3[b],v.at[0])

class Reduce:
    def __init__(self, net, sin, sout, axes, base=0):
        self.net, self.sin, self.sout, self.axes = net, sin, sout, axes
        self.at=base; self.so=base; self.k=0
    def start(self, value):
        self.value=value
        self._send()
    def _send(self):
        a=self.axes[self.k]
        self.sout[self.so]=self.value
        sk=self.net.sender(self.sin.at[pl.ds(self.at,len(a))]); self.rk=self.net.taker()
        for i,d in enumerate(a): self.net.put(self.sout.at[self.so],self.sin.at[self.at+i],d,sk,self.rk)
    def step(self):
        n=len(self.axes[self.k])
        self.net.take(self.rk,self.sin.at[pl.ds(self.at,n)])
        for i in range(n): self.value=self.value+self.sin[self.at+i]
        self.at+=n; self.so+=1; self.k+=1
        if self.k<len(self.axes): self._send()
    def finish(self):
        while self.k<len(self.axes): self.step()
        return self.value
def rep(v): return jnp.broadcast_to(v,(8,128))

def first_kernel(pa, pb, prior, r0, va, vb, npl, *s):
    sc=s[:-4]; sin,sout,ssem,rsem=s[-4:]
    y,z,c,r=place(); mate=dev(y,z,1-c,r)
    ry=Ring(y,lambda i:dev(i,z,c,r)); rz=Ring(z,lambda i:dev(y,i,c,r))
    greet([mate]+ry.peers()+rz.peers())
    net=Net(ssem,rsem)
    t=reduce_tiles(net,mate,c,ry,rz,pa,pb,sc)
    res=prior[...]*t.T
    v=(prior[...]*res).astype(bf16)
    va[c,z,y]=v[0:128]; vb[c,y,z]=v[128:256]
    red=Reduce(net,sin,sout,[ry.peers(),rz.peers(),[mate]])
    def tick(k):
        if k==0:
            r0[...]=res
            red.start(rep(jnp.sum(res*res,axis=0,keepdims=True)))
        elif k>1: red.step()
    gather_tiles(net,mate,c,ry,rz,va,vb,tick)
    npl[...]=red.finish()
    net.drain()
    assert (net.ns,net.nr)==FIRST_NET, (net.ns,net.nr)

def mid_kernel(pa, pb, prior, r0, nrm, wi, r1, d1, it, nn, va, vb, dd, *s):
    sc=s[:-4]; sin,sout,ssem,rsem=s[-4:]
    y,z,c,r=place(); mate=dev(y,z,1-c,r)
    ry=Ring(y,lambda i:dev(i,z,c,r)); rz=Ring(z,lambda i:dev(y,i,c,r)); rx=Ring(r,lambda i:dev(y,z,c,i))
    here=rx.peers()+[mate]+[dev(y,z,1-c,x) for x in rx.to[1:]]
    greet(here+ry.peers()+rz.peers())
    net=Net(ssem,rsem)
    plane=[ry.peers(),rz.peers(),[mate]]
    ra=Reduce(net,sin,sout,plane,0)
    def tick(k):
        if k==0: ra.start(wi[...])
        else: ra.step()
    t=reduce_tiles(net,mate,c,ry,rz,pa,pb,sc,tick)
    n0=nrm[0:1]
    step=n0/(n0+ra.finish()[0:1])
    d0=r0[...]
    res=d0-step*(d0+prior[...]*t.T)
    rb=Reduce(net,sin,sout,[here,ry.peers(),rz.peers()],7)
    rb.start(rep(jnp.sum(res*res,axis=0,keepdims=True)))
    it[...]=step*d0
    r1[...]=res
    n1=rb.finish()
    nn[...]=n1
    d=res+(n1[0:1]/n0)*d0
    v=(prior[...]*d).astype(bf16)
    va[c,z,y]=v[0:128]; vb[c,y,z]=v[128:256]
    rc=Reduce(net,sin,sout,plane,20)
    def tick2(k):
        if k==0:
            d1[...]=d
            rc.start(rep(jnp.sum(d*d,axis=0,keepdims=True)))
        elif k>1: rc.step()
    gather_tiles(net,mate,c,ry,rz,va,vb,tick2)
    dd[...]=rc.finish()
    net.drain()
    assert (net.ns,net.nr)==MID_NET, (net.ns,net.nr)

def last_kernel(pa, pb, n1, dd, wi, back, step, *s):
    sc=s[:-4]; sin,sout,ssem,rsem=s[-4:]
    y,z,c,r=place(); mate=dev(y,z,1-c,r)
    ry=Ring(y,lambda i:dev(i,z,c,r)); rz=Ring(z,lambda i:dev(y,i,c,r))
    greet([mate]+ry.peers()+rz.peers())
    net=Net(ssem,rsem)
    ra=Reduce(net,sin,sout,[ry.peers(),rz.peers(),[mate]],0)
    def tick(k):
        if k==0: ra.start(wi[...])
        else: ra.step()
    t=reduce_tiles(net,mate,c,ry,rz,pa,pb,sc,tick)
    step[...]=n1[...]/(dd[...]+ra.finish())
    back[...]=t.T
    net.drain()
    assert (net.ns,net.nr)==LAST_NET, (net.ns,net.nr)

CH=4
def cross_kernel(img, wgt, part, w, tot, wi, g, sin, sout, ssem, rsem):
    y,z,c,r=place()
    rx=Ring(r,lambda i:dev(y,z,c,i))
    greet(rx.peers())
    net=Net(ssem,rsem)
    n=8//CH
    B=[pl.ds(j*n,n) for j in range(CH)]
    s1=net.sender(g); k1=[net.taker() for j in range(CH)]
    for j in range(CH):
        for d in FAR: net.put(img.at[rx.to[d],B[j]],g.at[d-1,B[j]],rx.dev[d],s1,k1[j])
    ra=Reduce(net,sin,sout,[rx.peers()],0)
    ra.start(part[...])
    sums=jnp.zeros((64,128),f32)
    s2=net.sender(g); k2=net.taker()
    for j in range(CH):
        b=B[j]
        x=img[r,b].astype(f32)
        net.take(k1[j],g.at[pl.ds(0,3),pl.ds(0,n)])
        x=x+(g[0,b].astype(f32)+g[1,b].astype(f32)+g[2,b].astype(f32))
        m=wgt[b]*x
        w[r,b]=m.astype(bf16)
        s=w.at[r,b]
        for d in FAR: net.put(s,s,rx.dev[d],s2,k2)
        sums=sums+jnp.sum(m*x,axis=0)
    rb=Reduce(net,sin,sout,[rx.peers()],3)
    rb.start(rep(jnp.sum(sums,axis=0,keepdims=True)))
    tot[...]=ra.finish()
    wi[...]=rb.finish()
    net.take(k2,g)
    net.drain()
    assert (net.ns,net.nr)==CROSS_NET, (net.ns,net.nr)

FIRST_NET=(15,37); MID_NET=(21,43); LAST_NET=(9,21); CROSS_NET=(4,CH+3)
def _call(kernel, outs, scratch, cid, lim, name, *args):
    return pl.pallas_call(kernel,out_shape=outs,in_specs=[VM]*len(args),out_specs=tuple([VM]*len(outs)),
        scratch_shapes=scratch,compiler_params=pltpu.CompilerParams(collective_id=cid,has_side_effects=True,vmem_limit_bytes=lim<<20),name=name)(*args)
VA=SH((2,4,4,128,128),bf16); ROW=SH((8,128)); TILE=SH((256,128))
def tail(n, net): return [pltpu.VMEM((n,8,128),f32)]*2+[pltpu.SemaphoreType.DMA((k,)) for k in net]
def first(pa,pb,prior):
    return _call(first_kernel,[TILE,VA,VA,ROW],reduce_scratch(f32,f32)+tail(7,FIRST_NET),0,22,"first",pa,pb,prior)
def mid(pa,pb,prior,r0,nrm,wi):
    return _call(mid_kernel,[TILE,TILE,TILE,ROW,VA,VA,ROW],reduce_scratch(bf16,pa.dtype)+tail(27,MID_NET),1,18,"mid",pa,pb,prior,r0,nrm,wi)
def last(pa,pb,n1,dd,wi):
    return _call(last_kernel,[TILE,ROW],reduce_scratch(bf16,pa.dtype)+tail(7,LAST_NET),2,14,"last",pa,pb,n1,dd,wi)
def cross(img,wgt,part):
    return _call(cross_kernel,[SH((4,8,64,128),bf16),ROW,ROW],[pltpu.VMEM((3,8,64,128),bf16)]+tail(6,CROSS_NET),3,8,"cross",img.reshape(4,8,64,128),wgt,part)

def per_device(footprints, block_sounding, block_tile, block_count, observations, obs_weight, prior_std):
    F = footprints
    plan, w0, wgt, prior = begin(block_count, block_sounding, block_tile, observations, obs_weight, prior_std.reshape(1, 256))
    pa, pb = transpose_map(plan, F, w0, f32)
    r0, va, vb, norm = first(pa, pb, prior)
    img = forward_map(plan, F, va, vb)
    w, norm, wi = cross(img, wgt, norm)
    pa, pb = transpose_map(plan, F, w.reshape(32, 64, 128), f32)
    r1, d1, it, n1, va, vb, dd = mid(pa, pb, prior, r0, norm, wi)
    img = forward_map(plan, F, va, vb)
    w, dd, wi = cross(img, wgt, dd)
    pa, pb = transpose_map(plan, F, w.reshape(32, 64, 128), bf16)
    back, step = last(pa, pb, n1, dd, wi)
    step = step[0:1]
    resid = r1 - step * (d1 + prior * back)
    flux = prior * (it + step * d1)
    return flux[None, None], resid[None, None]


def solution(mesh):
    return jax.shard_map(
        per_device,
        mesh=mesh,
        in_specs=(
            P(("orbit", "region"), None, None),
            P(("orbit", "region")),
            P(("orbit", "region")),
            P(("orbit", "region")),
            P("orbit", None, None),
            P("orbit", None),
            P("region", "orbit", None),
        ),
        out_specs=(P("region", "orbit", None, None), P("region", "orbit", None, None)),
        check_vma=False,
    )
```

```python
import jax
import jax.numpy as jnp
from jax import lax
from jax.experimental import pallas as pl
from jax.experimental.pallas import tpu as pltpu
from jax.sharding import PartitionSpec as P

f32 = jnp.float32
bf16 = jnp.bfloat16
def SH(shape, dtype=f32): return jax.ShapeDtypeStruct(shape, dtype)

NB=320; NBP=384; NSLOT=512; UN=24; NCH=4

def sort_blocks(n, bt_row, bt_col, bs_col):
    iota=lambda shape,d: lax.broadcasted_iota(jnp.int32, shape, d)
    trow=jnp.where(iota((1,NBP),1)<n, bt_row, 32.0)
    live=iota((NBP,1),0)<n
    tcol=jnp.where(live, bt_col, 32.0)
    same=(trow==tcol)&(iota((NBP,NBP),1)<iota((NBP,NBP),0))
    rank=jnp.sum(jnp.where(same,1.0,0.0),axis=1,keepdims=True)
    lane=iota((NBP,128),1); lanef=lane.astype(f32)
    num=jnp.sum(jnp.where((tcol==lanef)&(lane<32),1.0,0.0),axis=0,keepdims=True)
    g=jnp.floor((num+3.0)*0.25)
    start=jnp.sum(jnp.where(lanef<tcol,jnp.broadcast_to(g,(NBP,128)),0.0),axis=1,keepdims=True)
    pos=jnp.where(live,4.0*start+rank,-1.0).astype(jnp.int32)
    ident=iota((NBP,1),0).astype(f32)*64.0+bs_col+1.0
    hit=pos==iota((NBP,NSLOT),1)
    slots=jnp.sum(jnp.where(hit,jnp.broadcast_to(ident,(NBP,NSLOT)),0.0),axis=0,keepdims=True)
    l2=iota((128,128),1); s2=iota((128,128),0)
    gend=jnp.sum(jnp.where(l2<=s2,jnp.broadcast_to(g,(128,128)),0.0),axis=1,keepdims=True)
    gt=jnp.sum(jnp.where((s2<32)&(gend<=l2.astype(f32)),1.0,0.0),axis=0,keepdims=True)
    total=jnp.sum(g,axis=1,keepdims=True)
    return slots, jnp.where(iota((1,128),1)==127,jnp.broadcast_to(total,(1,128)),gt)

def sort_kernel(cnt, packed, plan):
    p=packed[...].astype(f32)
    q=p.T
    slots,gt=sort_blocks(cnt[0],p[0:1],q[:,0:1],q[:,1:2])
    plan[0:1]=slots.astype(jnp.int32)
    plan[1:2,0:128]=gt.astype(jnp.int32)

def spread_kernel(obs, weight, prior, w0, wgt, pri):
    pri[...]=jnp.broadcast_to(prior[...],(128,256)).T
    own=pl.multiple_of(8*lax.axis_index("region"),8)
    def spread(x): return jnp.broadcast_to(x,(128,64)).T
    mine=weight[pl.ds(own,8)]
    for k in range(8):
        wgt[k]=spread(mine[k:k+1])
    every=weight[...]
    for k in range(32):
        w0[k]=(spread(every[k:k+1])*obs[k]).astype(bf16)

SM=pl.BlockSpec(memory_space=pltpu.SMEM); VM=pl.BlockSpec(memory_space=pltpu.VMEM)
def begin(cnt, bs, bt, obs, weight, prior):
    packed=jnp.pad(jnp.stack([bt,bs]),((0,6),(0,NBP-NB)))
    plan=pl.pallas_call(sort_kernel,out_shape=SH((2,NSLOT),jnp.int32),in_specs=[SM,VM],out_specs=VM,
        cost_estimate=pl.CostEstimate(flops=10**10,bytes_accessed=3*10**7,transcendentals=0),
        compiler_params=pltpu.CompilerParams(vmem_limit_bytes=8<<20),name="sort")(cnt,packed)
    w0,wgt,pri=pl.pallas_call(spread_kernel,out_shape=(SH((32,64,128),bf16),SH((8,64,128)),SH((256,128))),
        in_specs=[VM]*3,out_specs=(VM,)*3,
        cost_estimate=pl.CostEstimate(flops=10**9,bytes_accessed=4*10**6,transcendentals=0),
        compiler_params=pltpu.CompilerParams(vmem_limit_bytes=8<<20),name="spread")(obs,weight,prior)
    return plan,w0,wgt,pri

def snd(plan,g,k):
    v=plan[0,4*g+k]
    return jnp.where(v==0,32,jnp.bitwise_and(v-1,63))
def group_loop(plan, body):
    turns=(plan[1,127]+(UN-1))//UN
    def turn(i,c):
        body(i)
        return c
    lax.fori_loop(0,turns,turn,0)
def four(plan,F,g):
    out=[]
    for k in range(4):
        v=plan[0,4*g+k]
        out.append(F[lax.shift_right_logical(jnp.maximum(v-1,0),6)])
    return jnp.concatenate(out,axis=0)

def t_kernel(plan, F, w, pa, pb, acc, wt0, wt1):
    lane=lax.broadcasted_iota(jnp.int32,(128,128),1)
    for p in range(16):
        x=jnp.concatenate([w[2*p],w[2*p+1]],axis=0).astype(f32).T
        y=pltpu.roll(x,64,1)
        lo=lane<64
        z=jnp.zeros_like(x)
        wt0[2*p]=jnp.where(lo,x,z).astype(bf16)
        wt1[2*p]=jnp.where(lo,z,y).astype(bf16)
        wt0[2*p+1]=jnp.where(lo,y,z).astype(bf16)
        wt1[2*p+1]=jnp.where(lo,z,x).astype(bf16)
    wt0[32]=jnp.zeros((128,128),bf16)
    wt1[32]=jnp.zeros((128,128),bf16)
    acc[...]=jnp.zeros_like(acc)
    def body(i):
        for j in range(UN):
            g=i*UN+j
            s=[snd(plan,g,k) for k in range(4)]
            lhs=jnp.concatenate([wt0[s[0]]+wt1[s[1]],wt0[s[2]]+wt1[s[3]]],axis=1)
            acc[plan[1,g]]+=jnp.dot(lhs,four(plan,F,g),preferred_element_type=f32)
    group_loop(plan,body)
    for y in range(4):
        for z in range(4):
            for c in range(2):
                x=acc[(y*4+z)*2+c].astype(pa.dtype)
                pa[c,z,y]=x[0:64]
                pb[c,y,z]=x[64:128]
def transpose_map(plan, F, w, dtype):
    o=SH((2,4,4,64,256),dtype)
    return pl.pallas_call(t_kernel,out_shape=(o,o),in_specs=[SM,VM,VM],out_specs=(VM,VM),
        scratch_shapes=[pltpu.VMEM((33,128,256),f32),pltpu.VMEM((33,128,128),bf16),pltpu.VMEM((33,128,128),bf16)],
        compiler_params=pltpu.CompilerParams(vmem_limit_bytes=24<<20), name="tmap")(plan,F,w)

def f_kernel(plan, F, va, vb, img, acc):
    acc[...]=jnp.zeros_like(acc)
    def body(i):
        for j in range(UN):
            g=i*UN+j
            t=jnp.minimum(plan[1,g],31)
            c=jnp.bitwise_and(t,1); z=jnp.bitwise_and(lax.shift_right_logical(t,1),3); y=lax.shift_right_logical(t,3)
            rhs=jnp.concatenate([va[c,z*4+y],vb[c,y*4+z]],axis=0)
            out=jnp.dot(four(plan,F,g),rhs,preferred_element_type=f32)
            for k in range(4):
                acc[snd(plan,g,k)]+=out[64*k:64*k+64]
    group_loop(plan,body)
    img[...]=acc[0:32].astype(img.dtype)
def forward_map(plan, F, va, vb):
    return pl.pallas_call(f_kernel,out_shape=SH((32,64,128),bf16),in_specs=[SM,VM,VM,VM],out_specs=VM,
        scratch_shapes=[pltpu.VMEM((33,64,128),f32)],
        compiler_params=pltpu.CompilerParams(vmem_limit_bytes=18<<20), name="fmap")(plan,F,va.reshape(2,16,128,128),vb.reshape(2,16,128,128))

MESH=pl.DeviceIdType.MESH
class Net:
    def __init__(self, send, recv):
        self.send, self.recv, self.ns, self.nr, self.owed = send, recv, 0, 0, []
    def sender(self, whole):
        k=self.ns; self.ns+=1
        self.owed.append((k,whole))
        return k
    def taker(self):
        k=self.nr; self.nr+=1
        return k
    def put(self, src, dst, dev, sk, rk):
        pltpu.make_async_remote_copy(src_ref=src,dst_ref=dst,send_sem=self.send.at[sk],recv_sem=self.recv.at[rk],device_id=dev,device_id_type=MESH).start()
    def take(self, rk, whole):
        pltpu.make_async_copy(whole,whole,self.recv.at[rk]).wait()
    def drain(self):
        for k,whole in self.owed:
            pltpu.make_async_copy(whole,whole,self.send.at[k]).wait()

def place():
    o=lax.axis_index("orbit"); r=lax.axis_index("region")
    return o//8,(o//2)%4,o%2,r
def dev(y,z,c,r): return (y*8+z*2+c, r)
def greet(devs):
    bar=pltpu.get_barrier_semaphore()
    for d in devs:
        pl.semaphore_signal(bar,inc=1,device_id=d,device_id_type=MESH)
    pl.semaphore_wait(bar,len(devs))

class Ring:
    def __init__(self, i, at):
        self.i=i
        self.to=[(i+d)%4 for d in range(4)]
        self.dev=[at((i+d)%4) for d in range(4)]
    def peers(self): return self.dev[1:4]
FAR=(1,3,2)

def reduce_scratch(dt, cdt):
    V=pltpu.VMEM
    return [V((4,4,64,256),cdt)]*2+[V((4,4,64,256),dt)]*2+[V((3,4,64,256),dt)]*2+[V((3,64,256),dt)]*4

def reduce_tiles(net, mate, c, ry, rz, pa, pb, sc, tick=lambda k:None):
    ra,rb,qa,qb,ga,gb,sa,sb,ha,hb=sc
    sides=((ry,rz,pa,ra,qa,ga,sa,ha),(rz,ry,pb,rb,qb,gb,sb,hb))
    order=(2,1,3,0)
    s0=[net.sender(r) for (m,n,p,r,q,g,s,h) in sides]
    k0=[[net.taker() for x in sides] for e in order]
    for k,e in enumerate(order):
        for b,(m,n,p,r,q,g,s,h) in enumerate(sides):
            net.put(p.at[1-c,n.to[e]],r.at[n.to[e]],mate,s0[b],k0[k][b])
    tick(0)
    s1=[net.sender(g) for (m,n,p,r,q,g,s,h) in sides]
    k1=[[net.taker() for x in sides] for e in order]
    for k,e in enumerate(order):
        for b,(m,n,p,r,q,g,s,h) in enumerate(sides):
            j=n.to[e]
            net.take(k0[k][b],r.at[j])
            for d in FAR:
                q[j,m.to[d]]=(p[c,j,m.to[d]].astype(f32)+r[j,m.to[d]].astype(f32)).astype(q.dtype)
                net.put(q.at[j,m.to[d]],g.at[d-1,j],m.dev[d],s1[b],k1[k][b])
    tick(1)
    s2=[net.sender(s) for (m,n,p,r,q,g,s,h) in sides]
    k2=[net.taker() for x in sides]
    own=[None,None]
    for k,e in enumerate(order):
        for b,(m,n,p,r,q,g,s,h) in enumerate(sides):
            j=n.to[e]
            x=p[c,j,m.i].astype(f32)+r[j,m.i].astype(f32)
            net.take(k1[k][b],h)
            x=x+(g[0,j].astype(f32)+g[1,j].astype(f32)+g[2,j].astype(f32))
            if e:
                s[e-1]=x.astype(s.dtype)
                net.put(s.at[e-1],h.at[e-1],n.dev[e],s2[b],k2[b])
            else: own[b]=x
    tick(2)
    for b,(m,n,p,r,q,g,s,h) in enumerate(sides):
        net.take(k2[b],h)
        own[b]=own[b]+(h[0].astype(f32)+h[1].astype(f32)+h[2].astype(f32))
    return jnp.concatenate(own,axis=0)

def gather_tiles(net, mate, c, ry, rz, va, vb, tick=lambda k:None):
    sides=((ry,rz,va),(rz,ry,vb))
    three=[v.at[0,0,pl.ds(0,3)] for m,n,v in sides]
    s1=[net.sender(x) for x in three]
    k1=[[net.taker() for d in range(3)] for x in sides]
    for b,(m,n,v) in enumerate(sides):
        s=v.at[c,n.i,m.i]
        for d in (1,3,2): net.put(s,s,n.dev[d],s1[b],k1[b][d-1])
    tick(0)
    s2=[net.sender(v.at[0,pl.ds(0,3)]) for m,n,v in sides]
    order=(0,3,1,2)
    k2=[[net.taker() for x in sides] for e in order]
    for k,e in enumerate(order):
        for b,(m,n,v) in enumerate(sides):
            s=v.at[c,n.to[e],m.i]
            if e: net.take(k1[b][3-e],s)
            for d in FAR: net.put(s,s,m.dev[d],s2[b],k2[k][b])
    tick(1)
    s3=[net.sender(v.at[0]) for m,n,v in sides]
    k3=[net.taker() for x in sides]
    for k,e in enumerate(order):
        for b,(m,n,v) in enumerate(sides):
            net.take(k2[k][b],three[b])
            s=v.at[c,n.to[e]]
            net.put(s,s,mate,s3[b],k3[b])
        if k==1: tick(2)
    tick(3)
    for b,(m,n,v) in enumerate(sides): net.take(k3[b],v.at[0])

class Reduce:
    def __init__(self, net, sin, sout, axes, base=0):
        self.net, self.sin, self.sout, self.axes = net, sin, sout, axes
        self.at=base; self.so=base; self.k=0
    def start(self, value):
        self.value=value
        self._send()
    def _send(self):
        a=self.axes[self.k]
        self.sout[self.so]=self.value
        sk=self.net.sender(self.sin.at[pl.ds(self.at,len(a))]); self.rk=self.net.taker()
        for i,d in enumerate(a): self.net.put(self.sout.at[self.so],self.sin.at[self.at+i],d,sk,self.rk)
    def step(self):
        n=len(self.axes[self.k])
        self.net.take(self.rk,self.sin.at[pl.ds(self.at,n)])
        for i in range(n): self.value=self.value+self.sin[self.at+i]
        self.at+=n; self.so+=1; self.k+=1
        if self.k<len(self.axes): self._send()
    def finish(self):
        while self.k<len(self.axes): self.step()
        return self.value
def rep(v): return jnp.broadcast_to(v,(8,128))

def first_kernel(pa, pb, prior, r0, va, vb, npl, *s):
    sc=s[:-4]; sin,sout,ssem,rsem=s[-4:]
    y,z,c,r=place(); mate=dev(y,z,1-c,r)
    ry=Ring(y,lambda i:dev(i,z,c,r)); rz=Ring(z,lambda i:dev(y,i,c,r))
    greet([mate]+ry.peers()+rz.peers())
    net=Net(ssem,rsem)
    t=reduce_tiles(net,mate,c,ry,rz,pa,pb,sc)
    res=prior[...]*t.T
    v=(prior[...]*res).astype(bf16)
    va[c,z,y]=v[0:128]; vb[c,y,z]=v[128:256]
    red=Reduce(net,sin,sout,[ry.peers(),rz.peers(),[mate]])
    def tick(k):
        if k==0:
            r0[...]=res
            red.start(rep(jnp.sum(res*res,axis=0,keepdims=True)))
        elif k>1: red.step()
    gather_tiles(net,mate,c,ry,rz,va,vb,tick)
    npl[...]=red.finish()
    net.drain()
    assert (net.ns,net.nr)==FIRST_NET, (net.ns,net.nr)

def mid_kernel(pa, pb, prior, r0, nrm, wi, r1, it, va, vb, two, *s):
    sc=s[:-4]; sin,sout,ssem,rsem=s[-4:]
    y,z,c,r=place(); mate=dev(y,z,1-c,r)
    ry=Ring(y,lambda i:dev(i,z,c,r)); rz=Ring(z,lambda i:dev(y,i,c,r))
    greet([mate]+ry.peers()+rz.peers())
    net=Net(ssem,rsem)
    plane=[ry.peers(),rz.peers(),[mate]]
    ra=Reduce(net,sin,sout,plane,0)
    def tick(k):
        if k==0: ra.start(wi[...])
        else: ra.step()
    t=reduce_tiles(net,mate,c,ry,rz,pa,pb,sc,tick)
    n0=nrm[0:1]
    step=n0/(n0+ra.finish()[0:1])
    d0=r0[...]
    res=d0-step*(d0+prior[...]*t.T)
    v=(prior[...]*res).astype(bf16)
    va[c,z,y]=v[0:128]; vb[c,y,z]=v[128:256]
    rc=Reduce(net,sin,sout,plane,7)
    def tick2(k):
        if k==0:
            it[...]=step*d0
            r1[...]=res
            first_row=lax.broadcasted_iota(jnp.int32,(8,128),0)==0
            rc.start(jnp.where(first_row,rep(jnp.sum(res*res,axis=0,keepdims=True)),rep(jnp.sum(res*d0,axis=0,keepdims=True))))
        elif k>1: rc.step()
    gather_tiles(net,mate,c,ry,rz,va,vb,tick2)
    two[...]=rc.finish()
    net.drain()
    assert (net.ns,net.nr)==MID_NET, (net.ns,net.nr)

def last_kernel(pa, pb, top, low, wi, back, step, *s):
    sc=s[:-4]; sin,sout,ssem,rsem=s[-4:]
    y,z,c,r=place(); mate=dev(y,z,1-c,r)
    ry=Ring(y,lambda i:dev(i,z,c,r)); rz=Ring(z,lambda i:dev(y,i,c,r))
    greet([mate]+ry.peers()+rz.peers())
    net=Net(ssem,rsem)
    ra=Reduce(net,sin,sout,[ry.peers(),rz.peers(),[mate]],0)
    def tick(k):
        if k==0: ra.start(wi[...])
        else: ra.step()
    t=reduce_tiles(net,mate,c,ry,rz,pa,pb,sc,tick)
    step[...]=top[...]/(low[...]+ra.finish())
    back[...]=t.T
    net.drain()
    assert (net.ns,net.nr)==LAST_NET, (net.ns,net.nr)

CH=4
def exchange(img, wgt, w, sin, sout, ssem, rsem, g, part, keep, base):
    y,z,c,r=place()
    rx=Ring(r,lambda i:dev(y,z,c,i))
    greet(rx.peers())
    net=Net(ssem,rsem)
    n=8//CH
    B=[pl.ds(j*n,n) for j in range(CH)]
    s1=net.sender(g); k1=[net.taker() for j in range(CH)]
    ra=Reduce(net,sin,sout,[rx.peers()],0)
    ra.start(part)
    for j in range(CH):
        for d in FAR: net.put(img.at[rx.to[d],B[j]],g.at[d-1,B[j]],rx.dev[d],s1,k1[j])
    sums=jnp.zeros((64,128),f32)
    s2=net.sender(g); k2=net.taker()
    extra=base(ra.finish())
    for j in range(CH):
        b=B[j]
        x=img[r,b].astype(f32)
        net.take(k1[j],g.at[pl.ds(0,3),pl.ds(0,n)])
        x=extra(b,x+(g[0,b].astype(f32)+g[1,b].astype(f32)+g[2,b].astype(f32)))
        keep(b,x)
        m=wgt[b]*x
        w[r,b]=m.astype(bf16)
        s=w.at[r,b]
        for d in FAR: net.put(s,s,rx.dev[d],s2,k2)
        sums=sums+jnp.sum(m*x,axis=0)
    rb=Reduce(net,sin,sout,[rx.peers()],3)
    rb.start(rep(jnp.sum(sums,axis=0,keepdims=True)))
    wi=rb.finish()
    net.take(k2,g)
    net.drain()
    assert (net.ns,net.nr)==CROSS_NET, (net.ns,net.nr)
    return wi

def cross_kernel(img, wgt, part, w, tot, wi, image, g, sin, sout, ssem, rsem):
    def base(total):
        tot[...]=total
        return lambda b,x: x
    def keep(b,x): image[b]=x
    wi[...]=exchange(img,wgt,w,sin,sout,ssem,rsem,g,part[...],keep,base)

def again_kernel(img, wgt, part, n0, image, w, low, top, beta, wi, g, sin, sout, ssem, rsem):
    def base(total):
        n1=total[0:1]
        ratio=n1/n0[0:1]
        top[...]=rep(n1)
        beta[...]=rep(ratio)
        low[...]=rep(n1+ratio*(2.0*total[1:2]+ratio*n0[0:1]))
        return lambda b,x: x+ratio*image[b]
    wi[...]=exchange(img,wgt,w,sin,sout,ssem,rsem,g,part[...],lambda b,x:None,base)

FIRST_NET=(15,37); MID_NET=(18,40); LAST_NET=(9,21); CROSS_NET=(4,CH+3)
def _call(kernel, outs, scratch, cid, lim, name, *args):
    return pl.pallas_call(kernel,out_shape=outs,in_specs=[VM]*len(args),out_specs=tuple([VM]*len(outs)),
        scratch_shapes=scratch,compiler_params=pltpu.CompilerParams(collective_id=cid,has_side_effects=True,vmem_limit_bytes=lim<<20),name=name)(*args)
VA=SH((2,4,4,128,128),bf16); ROW=SH((8,128)); TILE=SH((256,128))
def tail(n, net): return [pltpu.VMEM((n,8,128),f32)]*2+[pltpu.SemaphoreType.DMA((k,)) for k in net]
def first(pa,pb,prior):
    return _call(first_kernel,[TILE,VA,VA,ROW],reduce_scratch(f32,f32)+tail(7,FIRST_NET),0,22,"first",pa,pb,prior)
def mid(pa,pb,prior,r0,nrm,wi):
    return _call(mid_kernel,[TILE,TILE,VA,VA,ROW],reduce_scratch(bf16,pa.dtype)+tail(14,MID_NET),1,18,"mid",pa,pb,prior,r0,nrm,wi)
def last(pa,pb,top,low,wi):
    return _call(last_kernel,[TILE,ROW],reduce_scratch(bf16,pa.dtype)+tail(7,LAST_NET),2,14,"last",pa,pb,top,low,wi)
def cross(img,wgt,part):
    return _call(cross_kernel,[SH((4,8,64,128),bf16),ROW,ROW,SH((8,64,128))],[pltpu.VMEM((3,8,64,128),bf16)]+tail(6,CROSS_NET),3,8,"cross",img.reshape(4,8,64,128),wgt,part)
def again(img,wgt,part,n0,image):
    return _call(again_kernel,[SH((4,8,64,128),bf16),ROW,ROW,ROW,ROW],[pltpu.VMEM((3,8,64,128),bf16)]+tail(6,CROSS_NET),4,8,"again",img.reshape(4,8,64,128),wgt,part,n0,image)

def per_device(footprints, block_sounding, block_tile, block_count, observations, obs_weight, prior_std):
    F = footprints
    plan, w0, wgt, prior = begin(block_count, block_sounding, block_tile, observations, obs_weight, prior_std.reshape(1, 256))
    pa, pb = transpose_map(plan, F, w0, f32)
    r0, va, vb, norm = first(pa, pb, prior)
    img = forward_map(plan, F, va, vb)
    w, norm, wi, image = cross(img, wgt, norm)
    pa, pb = transpose_map(plan, F, w.reshape(32, 64, 128), f32)
    r1, it, va, vb, two = mid(pa, pb, prior, r0, norm, wi)
    img = forward_map(plan, F, va, vb)
    w, low, top, beta, wi = again(img, wgt, two, norm, image)
    pa, pb = transpose_map(plan, F, w.reshape(32, 64, 128), bf16)
    back, step = last(pa, pb, top, low, wi)
    step, beta = step[0:1], beta[0:1]
    d1 = r1 + beta * r0
    resid = r1 - step * (d1 + prior * back)
    flux = prior * (it + step * d1)
    return flux[None, None], resid[None, None]


def solution(mesh):
    return jax.shard_map(
        per_device,
        mesh=mesh,
        in_specs=(
            P(("orbit", "region"), None, None),
            P(("orbit", "region")),
            P(("orbit", "region")),
            P(("orbit", "region")),
            P("orbit", None, None),
            P("orbit", None),
            P("region", "orbit", None),
        ),
        out_specs=(P("region", "orbit", None, None), P("region", "orbit", None, None)),
        check_vma=False,
    )
```

```python
import jax
import jax.numpy as jnp
from jax import lax
from jax.experimental import pallas as pl
from jax.experimental.pallas import tpu as pltpu
from jax.sharding import PartitionSpec as P

f32 = jnp.float32
bf16 = jnp.bfloat16
def SH(shape, dtype=f32): return jax.ShapeDtypeStruct(shape, dtype)

NB=320; NBP=384; NSLOT=512; UN=24; NCH=4

def sort_blocks(n, bt_row, bt_col, bs_col):
    iota=lambda shape,d: lax.broadcasted_iota(jnp.int32, shape, d)
    trow=jnp.where(iota((1,NBP),1)<n, bt_row, 32.0)
    live=iota((NBP,1),0)<n
    tcol=jnp.where(live, bt_col, 32.0)
    same=(trow==tcol)&(iota((NBP,NBP),1)<iota((NBP,NBP),0))
    rank=jnp.sum(jnp.where(same,1.0,0.0),axis=1,keepdims=True)
    lane=iota((NBP,128),1); lanef=lane.astype(f32)
    num=jnp.sum(jnp.where((tcol==lanef)&(lane<32),1.0,0.0),axis=0,keepdims=True)
    g=jnp.floor((num+3.0)*0.25)
    start=jnp.sum(jnp.where(lanef<tcol,jnp.broadcast_to(g,(NBP,128)),0.0),axis=1,keepdims=True)
    pos=jnp.where(live,4.0*start+rank,-1.0).astype(jnp.int32)
    ident=iota((NBP,1),0).astype(f32)*64.0+bs_col+1.0
    hit=pos==iota((NBP,NSLOT),1)
    slots=jnp.sum(jnp.where(hit,jnp.broadcast_to(ident,(NBP,NSLOT)),0.0),axis=0,keepdims=True)
    l2=iota((128,128),1); s2=iota((128,128),0)
    gend=jnp.sum(jnp.where(l2<=s2,jnp.broadcast_to(g,(128,128)),0.0),axis=1,keepdims=True)
    gt=jnp.sum(jnp.where((s2<32)&(gend<=l2.astype(f32)),1.0,0.0),axis=0,keepdims=True)
    total=jnp.sum(g,axis=1,keepdims=True)
    return slots, jnp.where(iota((1,128),1)==127,jnp.broadcast_to(total,(1,128)),gt)

def sort_kernel(cnt, packed, plan):
    p=packed[...].astype(f32)
    q=p.T[:,0:1]
    tile=jnp.floor(q*(1.0/64.0))
    slots,gt=sort_blocks(cnt[0],jnp.floor(p[0:1]*(1.0/64.0)),tile,q-64.0*tile)
    plan[0:1]=slots.astype(jnp.int32)
    plan[1:2,0:128]=gt.astype(jnp.int32)

def spread_kernel(obs, weight, prior, w0, wgt, pri):
    pri[...]=jnp.broadcast_to(prior[...],(128,256)).T
    own=pl.multiple_of(8*lax.axis_index("region"),8)
    def spread(x): return jnp.broadcast_to(x,(128,64)).T
    mine=weight[pl.ds(own,8)]
    for k in range(8):
        wgt[k]=spread(mine[k:k+1])
    every=weight[...]
    for k in range(32):
        w0[k]=(spread(every[k:k+1])*obs[k]).astype(bf16)

SM=pl.BlockSpec(memory_space=pltpu.SMEM); VM=pl.BlockSpec(memory_space=pltpu.VMEM)
def begin(cnt, bs, bt, obs, weight, prior):
    packed=jnp.pad((bt*64+bs).reshape(1,NB),((0,7),(0,NBP-NB)))
    plan=pl.pallas_call(sort_kernel,out_shape=SH((2,NSLOT),jnp.int32),in_specs=[SM,VM],out_specs=VM,
        cost_estimate=pl.CostEstimate(flops=10**10,bytes_accessed=3*10**7,transcendentals=0),
        compiler_params=pltpu.CompilerParams(vmem_limit_bytes=8<<20),name="sort")(cnt,packed)
    w0,wgt,pri=pl.pallas_call(spread_kernel,out_shape=(SH((32,64,128),bf16),SH((8,64,128)),SH((256,128))),
        in_specs=[VM]*3,out_specs=(VM,)*3,
        cost_estimate=pl.CostEstimate(flops=10**9,bytes_accessed=4*10**6,transcendentals=0),
        compiler_params=pltpu.CompilerParams(vmem_limit_bytes=8<<20),name="spread")(obs,weight,prior)
    return plan,w0,wgt,pri

def snd(plan,g,k):
    v=plan[0,4*g+k]
    return jnp.where(v==0,32,jnp.bitwise_and(v-1,63))
def group_loop(plan, body):
    turns=(plan[1,127]+(UN-1))//UN
    def turn(i,c):
        body(i)
        return c
    lax.fori_loop(0,turns,turn,0)
def four(plan,F,g):
    out=[]
    for k in range(4):
        v=plan[0,4*g+k]
        out.append(F[lax.shift_right_logical(jnp.maximum(v-1,0),6)])
    return jnp.concatenate(out,axis=0)

def t_kernel(plan, F, w, pa, pb, acc, wt0, wt1):
    lane=lax.broadcasted_iota(jnp.int32,(128,128),1)
    for p in range(16):
        x=jnp.concatenate([w[2*p],w[2*p+1]],axis=0).astype(f32).T
        y=pltpu.roll(x,64,1)
        lo=lane<64
        z=jnp.zeros_like(x)
        wt0[2*p]=jnp.where(lo,x,z).astype(bf16)
        wt1[2*p]=jnp.where(lo,z,y).astype(bf16)
        wt0[2*p+1]=jnp.where(lo,y,z).astype(bf16)
        wt1[2*p+1]=jnp.where(lo,z,x).astype(bf16)
    wt0[32]=jnp.zeros((128,128),bf16)
    wt1[32]=jnp.zeros((128,128),bf16)
    acc[...]=jnp.zeros_like(acc)
    def body(i):
        for j in range(UN):
            g=i*UN+j
            s=[snd(plan,g,k) for k in range(4)]
            lhs=jnp.concatenate([wt0[s[0]]+wt1[s[1]],wt0[s[2]]+wt1[s[3]]],axis=1)
            acc[plan[1,g]]+=jnp.dot(lhs,four(plan,F,g),preferred_element_type=f32)
    group_loop(plan,body)
    for y in range(4):
        for z in range(4):
            for c in range(2):
                x=acc[(y*4+z)*2+c].astype(pa.dtype)
                pa[c,z,y]=x[0:64]
                pb[c,y,z]=x[64:128]
def transpose_map(plan, F, w, dtype):
    o=SH((2,4,4,64,256),dtype)
    return pl.pallas_call(t_kernel,out_shape=(o,o),in_specs=[SM,VM,VM],out_specs=(VM,VM),
        scratch_shapes=[pltpu.VMEM((33,128,256),f32),pltpu.VMEM((33,128,128),bf16),pltpu.VMEM((33,128,128),bf16)],
        compiler_params=pltpu.CompilerParams(vmem_limit_bytes=24<<20), name="tmap")(plan,F,w)

def f_kernel(plan, F, va, vb, img, acc):
    acc[...]=jnp.zeros_like(acc)
    def body(i):
        for j in range(UN):
            g=i*UN+j
            t=jnp.minimum(plan[1,g],31)
            c=jnp.bitwise_and(t,1); z=jnp.bitwise_and(lax.shift_right_logical(t,1),3); y=lax.shift_right_logical(t,3)
            rhs=jnp.concatenate([va[c,z*4+y],vb[c,y*4+z]],axis=0)
            out=jnp.dot(four(plan,F,g),rhs,preferred_element_type=f32)
            for k in range(4):
                acc[snd(plan,g,k)]+=out[64*k:64*k+64]
    group_loop(plan,body)
    img[...]=acc[0:32].astype(img.dtype)
def forward_map(plan, F, va, vb):
    return pl.pallas_call(f_kernel,out_shape=SH((32,64,128),bf16),in_specs=[SM,VM,VM,VM],out_specs=VM,
        scratch_shapes=[pltpu.VMEM((33,64,128),f32)],
        compiler_params=pltpu.CompilerParams(vmem_limit_bytes=18<<20), name="fmap")(plan,F,va.reshape(2,16,128,128),vb.reshape(2,16,128,128))

MESH=pl.DeviceIdType.MESH
class Net:
    def __init__(self, send, recv):
        self.send, self.recv, self.ns, self.nr, self.owed = send, recv, 0, 0, []
    def sender(self, whole):
        k=self.ns; self.ns+=1
        self.owed.append((k,whole))
        return k
    def taker(self):
        k=self.nr; self.nr+=1
        return k
    def put(self, src, dst, dev, sk, rk):
        pltpu.make_async_remote_copy(src_ref=src,dst_ref=dst,send_sem=self.send.at[sk],recv_sem=self.recv.at[rk],device_id=dev,device_id_type=MESH).start()
    def take(self, rk, whole):
        pltpu.make_async_copy(whole,whole,self.recv.at[rk]).wait()
    def drain(self):
        for k,whole in self.owed:
            pltpu.make_async_copy(whole,whole,self.send.at[k]).wait()

def place():
    o=lax.axis_index("orbit"); r=lax.axis_index("region")
    return o//8,(o//2)%4,o%2,r
def dev(y,z,c,r): return (y*8+z*2+c, r)
def greet(devs):
    bar=pltpu.get_barrier_semaphore()
    for d in devs:
        pl.semaphore_signal(bar,inc=1,device_id=d,device_id_type=MESH)
    pl.semaphore_wait(bar,len(devs))

class Ring:
    def __init__(self, i, at):
        self.i=i
        self.to=[(i+d)%4 for d in range(4)]
        self.dev=[at((i+d)%4) for d in range(4)]
    def peers(self): return self.dev[1:4]
FAR=(1,3,2)

def reduce_scratch(dt, cdt, relays=0):
    V=pltpu.VMEM
    return [V((4,4,64,256),cdt)]*2+[V((4,4,64,256),dt)]*2+[V((3,4,64,256),dt)]*2+[V((3,64,256),dt)]*4+[V((relays,64,256),dt)]*(4 if relays else 0)

def reduce_tiles(net, mate, c, ry, rz, pa, pb, sc, tick=lambda k:None, relays=0):
    ra,rb,qa,qb,ga,gb,sa,sb,ha,hb=sc[:10]
    ia,ib,oa,ob=sc[10:] if relays else (None,)*4
    sides=((ry,rz,pa,ra,qa,ga,sa,ha),(rz,ry,pb,rb,qb,gb,sb,hb))
    inn=(ia,ib); out=(oa,ob)
    order=(2,1,3,0)
    way=lambda k: 1 if k%2==0 else 3
    s0=[net.sender(r) for (m,n,p,r,q,g,s,h) in sides]
    k0=[[net.taker() for x in sides] for e in order]
    for k,e in enumerate(order):
        for b,(m,n,p,r,q,g,s,h) in enumerate(sides):
            net.put(p.at[1-c,n.to[e]],r.at[n.to[e]],mate,s0[b],k0[k][b])
    tick(0)
    if relays<4: s1=[net.sender(g.at[pl.ds(0,3),pl.ds(0,4-relays)]) for (m,n,p,r,q,g,s,h) in sides]
    k1=[[net.taker() for x in sides] for e in order]
    if relays:
        sr=[net.sender(x) for x in inn]
        sn=[net.sender(g.at[pl.ds(0,2),pl.ds(0,relays)]) for (m,n,p,r,q,g,s,h) in sides]
        kr=[[net.taker() for x in sides] for k in range(relays)]
    for k,e in enumerate(order):
        for b,(m,n,p,r,q,g,s,h) in enumerate(sides):
            j=n.to[e]
            net.take(k0[k][b],r.at[j])
            for d in (2,4-way(k),way(k)) if k<relays else FAR:
                q[j,m.to[d]]=(p[c,j,m.to[d]].astype(f32)+r[j,m.to[d]].astype(f32)).astype(q.dtype)
                if k>=relays: net.put(q.at[j,m.to[d]],g.at[d-1,j],m.dev[d],s1[b],k1[k][b])
                elif d==2: net.put(q.at[j,m.to[d]],inn[b].at[k],m.dev[way(k)],sr[b],kr[k][b])
                elif d!=way(k): net.put(q.at[j,m.to[d]],g.at[d-1,j],m.dev[d],sn[b],k1[k][b])
    for k in range(relays):
        for b,(m,n,p,r,q,g,s,h) in enumerate(sides):
            j=n.to[order[k]]; w=way(k)
            net.take(kr[k][b],inn[b].at[k])
            out[b][k]=(q[j,m.to[w]].astype(f32)+inn[b][k].astype(f32)).astype(q.dtype)
            net.put(out[b].at[k],g.at[w-1,j],m.dev[w],sn[b],k1[k][b])
    tick(1)
    s2=[net.sender(s) for (m,n,p,r,q,g,s,h) in sides]
    k2=[net.taker() for x in sides]
    own=[None,None]
    for k,e in enumerate(order):
        for b,(m,n,p,r,q,g,s,h) in enumerate(sides):
            j=n.to[e]
            x=p[c,j,m.i].astype(f32)+r[j,m.i].astype(f32)
            if k<relays:
                net.take(k1[k][b],h.at[pl.ds(0,2)])
                x=x+(g[0,j].astype(f32)+g[2,j].astype(f32))
            else:
                net.take(k1[k][b],h)
                x=x+(g[0,j].astype(f32)+g[1,j].astype(f32)+g[2,j].astype(f32))
            if e:
                s[e-1]=x.astype(s.dtype)
                net.put(s.at[e-1],h.at[e-1],n.dev[e],s2[b],k2[b])
            else: own[b]=x
    tick(2)
    for b,(m,n,p,r,q,g,s,h) in enumerate(sides):
        net.take(k2[b],h)
        own[b]=own[b]+(h[0].astype(f32)+h[1].astype(f32)+h[2].astype(f32))
    return jnp.concatenate(own,axis=0)

def gather_tiles(net, mate, c, ry, rz, va, vb, tick=lambda k:None):
    sides=((ry,rz,va),(rz,ry,vb))
    three=[v.at[0,0,pl.ds(0,3)] for m,n,v in sides]
    s1=[net.sender(x) for x in three]
    k1=[[net.taker() for d in range(3)] for x in sides]
    for b,(m,n,v) in enumerate(sides):
        s=v.at[c,n.i,m.i]
        for d in (1,3,2): net.put(s,s,n.dev[d],s1[b],k1[b][d-1])
    tick(0)
    s2=[net.sender(v.at[0,pl.ds(0,3)]) for m,n,v in sides]
    order=(0,3,1,2)
    k2=[[net.taker() for x in sides] for e in order]
    for k,e in enumerate(order):
        for b,(m,n,v) in enumerate(sides):
            s=v.at[c,n.to[e],m.i]
            if e: net.take(k1[b][3-e],s)
            for d in FAR: net.put(s,s,m.dev[d],s2[b],k2[k][b])
    tick(1)
    s3=[net.sender(v.at[0]) for m,n,v in sides]
    k3=[net.taker() for x in sides]
    for k,e in enumerate(order):
        for b,(m,n,v) in enumerate(sides):
            net.take(k2[k][b],three[b])
            s=v.at[c,n.to[e]]
            net.put(s,s,mate,s3[b],k3[b])
        if k==1: tick(2)
    tick(3)
    for b,(m,n,v) in enumerate(sides): net.take(k3[b],v.at[0])

class Reduce:
    def __init__(self, net, sin, sout, axes, base=0):
        self.net, self.sin, self.sout, self.axes = net, sin, sout, axes
        self.at=base; self.so=base; self.k=0
    def start(self, value):
        self.value=value
        self._send()
    def _send(self):
        a=self.axes[self.k]
        self.sout[self.so]=self.value
        sk=self.net.sender(self.sin.at[pl.ds(self.at,len(a))]); self.rk=self.net.taker()
        for i,d in enumerate(a): self.net.put(self.sout.at[self.so],self.sin.at[self.at+i],d,sk,self.rk)
    def step(self):
        n=len(self.axes[self.k])
        self.net.take(self.rk,self.sin.at[pl.ds(self.at,n)])
        for i in range(n): self.value=self.value+self.sin[self.at+i]
        self.at+=n; self.so+=1; self.k+=1
        if self.k<len(self.axes): self._send()
    def finish(self):
        while self.k<len(self.axes): self.step()
        return self.value
def rep(v): return jnp.broadcast_to(v,(8,128))

def first_kernel(pa, pb, prior, r0, va, vb, npl, *s):
    sc=s[:-4]; sin,sout,ssem,rsem=s[-4:]
    y,z,c,r=place(); mate=dev(y,z,1-c,r)
    ry=Ring(y,lambda i:dev(i,z,c,r)); rz=Ring(z,lambda i:dev(y,i,c,r))
    greet([mate]+ry.peers()+rz.peers())
    net=Net(ssem,rsem)
    t=reduce_tiles(net,mate,c,ry,rz,pa,pb,sc,relays=RELAYS)
    res=prior[...]*t.T
    v=(prior[...]*res).astype(bf16)
    va[c,z,y]=v[0:128]; vb[c,y,z]=v[128:256]
    red=Reduce(net,sin,sout,[ry.peers(),rz.peers(),[mate]])
    def tick(k):
        if k==0:
            r0[...]=res
            red.start(rep(jnp.sum(res*res,axis=0,keepdims=True)))
        elif k>1: red.step()
    gather_tiles(net,mate,c,ry,rz,va,vb,tick)
    npl[...]=red.finish()
    net.drain()
    assert (net.ns,net.nr)==FIRST_NET, (net.ns,net.nr)

def mid_kernel(pa, pb, prior, r0, nrm, wi, r1, it, va, vb, two, *s):
    sc=s[:-4]; sin,sout,ssem,rsem=s[-4:]
    y,z,c,r=place(); mate=dev(y,z,1-c,r)
    ry=Ring(y,lambda i:dev(i,z,c,r)); rz=Ring(z,lambda i:dev(y,i,c,r))
    greet([mate]+ry.peers()+rz.peers())
    net=Net(ssem,rsem)
    plane=[ry.peers(),rz.peers(),[mate]]
    ra=Reduce(net,sin,sout,plane,0)
    def tick(k):
        if k==0: ra.start(wi[...])
        else: ra.step()
    t=reduce_tiles(net,mate,c,ry,rz,pa,pb,sc,tick)
    n0=nrm[0:1]
    step=n0/(n0+ra.finish()[0:1])
    d0=r0[...]
    res=d0-step*(d0+prior[...]*t.T)
    v=(prior[...]*res).astype(bf16)
    va[c,z,y]=v[0:128]; vb[c,y,z]=v[128:256]
    rc=Reduce(net,sin,sout,plane,7)
    def tick2(k):
        if k==0:
            it[...]=step*d0
            r1[...]=res
            first_row=lax.broadcasted_iota(jnp.int32,(8,128),0)==0
            rc.start(jnp.where(first_row,rep(jnp.sum(res*res,axis=0,keepdims=True)),rep(jnp.sum(res*d0,axis=0,keepdims=True))))
        elif k>1: rc.step()
    gather_tiles(net,mate,c,ry,rz,va,vb,tick2)
    two[...]=rc.finish()
    net.drain()
    assert (net.ns,net.nr)==MID_NET, (net.ns,net.nr)

def last_kernel(pa, pb, top, low, wi, back, step, *s):
    sc=s[:-4]; sin,sout,ssem,rsem=s[-4:]
    y,z,c,r=place(); mate=dev(y,z,1-c,r)
    ry=Ring(y,lambda i:dev(i,z,c,r)); rz=Ring(z,lambda i:dev(y,i,c,r))
    greet([mate]+ry.peers()+rz.peers())
    net=Net(ssem,rsem)
    ra=Reduce(net,sin,sout,[ry.peers(),rz.peers(),[mate]],0)
    def tick(k):
        if k==0: ra.start(wi[...])
        else: ra.step()
    t=reduce_tiles(net,mate,c,ry,rz,pa,pb,sc,tick)
    step[...]=top[...]/(low[...]+ra.finish())
    back[...]=t.T
    net.drain()
    assert (net.ns,net.nr)==LAST_NET, (net.ns,net.nr)

CH=4
def exchange(img, wgt, w, sin, sout, ssem, rsem, g, part, keep, base):
    y,z,c,r=place()
    rx=Ring(r,lambda i:dev(y,z,c,i))
    greet(rx.peers())
    net=Net(ssem,rsem)
    n=8//CH
    B=[pl.ds(j*n,n) for j in range(CH)]
    s1=net.sender(g); k1=[net.taker() for j in range(CH)]
    ra=Reduce(net,sin,sout,[rx.peers()],0)
    ra.start(part)
    for j in range(CH):
        for d in FAR: net.put(img.at[rx.to[d],B[j]],g.at[d-1,B[j]],rx.dev[d],s1,k1[j])
    sums=jnp.zeros((64,128),f32)
    s2=net.sender(g); k2=net.taker()
    extra=base(ra.finish())
    for j in range(CH):
        b=B[j]
        x=img[r,b].astype(f32)
        net.take(k1[j],g.at[pl.ds(0,3),pl.ds(0,n)])
        x=extra(b,x+(g[0,b].astype(f32)+g[1,b].astype(f32)+g[2,b].astype(f32)))
        keep(b,x)
        m=wgt[b]*x
        w[r,b]=m.astype(bf16)
        s=w.at[r,b]
        for d in FAR: net.put(s,s,rx.dev[d],s2,k2)
        sums=sums+jnp.sum(m*x,axis=0)
    rb=Reduce(net,sin,sout,[rx.peers()],3)
    rb.start(rep(jnp.sum(sums,axis=0,keepdims=True)))
    wi=rb.finish()
    net.take(k2,g)
    net.drain()
    assert (net.ns,net.nr)==CROSS_NET, (net.ns,net.nr)
    return wi

def cross_kernel(img, wgt, part, w, tot, wi, image, g, sin, sout, ssem, rsem):
    def base(total):
        tot[...]=total
        return lambda b,x: x
    def keep(b,x): image[b]=x
    wi[...]=exchange(img,wgt,w,sin,sout,ssem,rsem,g,part[...],keep,base)

def again_kernel(img, wgt, part, n0, image, w, low, top, beta, wi, g, sin, sout, ssem, rsem):
    def base(total):
        n1=total[0:1]
        ratio=n1/n0[0:1]
        top[...]=rep(n1)
        beta[...]=rep(ratio)
        low[...]=rep(n1+ratio*(2.0*total[1:2]+ratio*n0[0:1]))
        return lambda b,x: x+ratio*image[b]
    wi[...]=exchange(img,wgt,w,sin,sout,ssem,rsem,g,part[...],lambda b,x:None,base)

RELAYS=4; FIRST_NET=(17,45); MID_NET=(18,40); LAST_NET=(9,21); CROSS_NET=(4,CH+3)
def _call(kernel, outs, scratch, cid, lim, name, *args):
    return pl.pallas_call(kernel,out_shape=outs,in_specs=[VM]*len(args),out_specs=tuple([VM]*len(outs)),
        scratch_shapes=scratch,compiler_params=pltpu.CompilerParams(collective_id=cid,has_side_effects=True,vmem_limit_bytes=lim<<20),name=name)(*args)
VA=SH((2,4,4,128,128),bf16); ROW=SH((8,128)); TILE=SH((256,128))
def tail(n, net): return [pltpu.VMEM((n,8,128),f32)]*2+[pltpu.SemaphoreType.DMA((k,)) for k in net]
def first(pa,pb,prior):
    return _call(first_kernel,[TILE,VA,VA,ROW],reduce_scratch(f32,f32,RELAYS)+tail(7,FIRST_NET),0,22,"first",pa,pb,prior)
def mid(pa,pb,prior,r0,nrm,wi):
    return _call(mid_kernel,[TILE,TILE,VA,VA,ROW],reduce_scratch(bf16,pa.dtype)+tail(14,MID_NET),1,18,"mid",pa,pb,prior,r0,nrm,wi)
def last(pa,pb,top,low,wi):
    return _call(last_kernel,[TILE,ROW],reduce_scratch(bf16,pa.dtype)+tail(7,LAST_NET),2,14,"last",pa,pb,top,low,wi)
def cross(img,wgt,part):
    return _call(cross_kernel,[SH((4,8,64,128),bf16),ROW,ROW,SH((8,64,128))],[pltpu.VMEM((3,8,64,128),bf16)]+tail(6,CROSS_NET),3,8,"cross",img.reshape(4,8,64,128),wgt,part)
def again(img,wgt,part,n0,image):
    return _call(again_kernel,[SH((4,8,64,128),bf16),ROW,ROW,ROW,ROW],[pltpu.VMEM((3,8,64,128),bf16)]+tail(6,CROSS_NET),4,8,"again",img.reshape(4,8,64,128),wgt,part,n0,image)

def per_device(footprints, block_sounding, block_tile, block_count, observations, obs_weight, prior_std):
    F = footprints
    plan, w0, wgt, prior = begin(block_count, block_sounding, block_tile, observations, obs_weight, prior_std.reshape(1, 256))
    pa, pb = transpose_map(plan, F, w0, f32)
    r0, va, vb, norm = first(pa, pb, prior)
    img = forward_map(plan, F, va, vb)
    w, norm, wi, image = cross(img, wgt, norm)
    pa, pb = transpose_map(plan, F, w.reshape(32, 64, 128), f32)
    r1, it, va, vb, two = mid(pa, pb, prior, r0, norm, wi)
    img = forward_map(plan, F, va, vb)
    w, low, top, beta, wi = again(img, wgt, two, norm, image)
    pa, pb = transpose_map(plan, F, w.reshape(32, 64, 128), bf16)
    back, step = last(pa, pb, top, low, wi)
    step, beta = step[0:1], beta[0:1]
    d1 = r1 + beta * r0
    resid = r1 - step * (d1 + prior * back)
    flux = prior * (it + step * d1)
    return flux[None, None], resid[None, None]


def solution(mesh):
    return jax.shard_map(
        per_device,
        mesh=mesh,
        in_specs=(
            P(("orbit", "region"), None, None),
            P(("orbit", "region")),
            P(("orbit", "region")),
            P(("orbit", "region")),
            P("orbit", None, None),
            P("orbit", None),
            P("region", "orbit", None),
        ),
        out_specs=(P("region", "orbit", None, None), P("region", "orbit", None, None)),
        check_vma=False,
    )
```

```python
import jax
import jax.numpy as jnp
from jax import lax
from jax.experimental import pallas as pl
from jax.experimental.pallas import tpu as pltpu
from jax.sharding import PartitionSpec as P

f32 = jnp.float32
bf16 = jnp.bfloat16
def SH(shape, dtype=f32): return jax.ShapeDtypeStruct(shape, dtype)

NB=320; NBP=384; NSLOT=512; UN=24; NCH=4

def sort_blocks(n, bt_row, bt_col, bs_col):
    iota=lambda shape,d: lax.broadcasted_iota(jnp.int32, shape, d)
    trow=jnp.where(iota((1,NBP),1)<n, bt_row, 32.0)
    live=iota((NBP,1),0)<n
    tcol=jnp.where(live, bt_col, 32.0)
    same=(trow==tcol)&(iota((NBP,NBP),1)<iota((NBP,NBP),0))
    rank=jnp.sum(jnp.where(same,1.0,0.0),axis=1,keepdims=True)
    lane=iota((NBP,128),1); lanef=lane.astype(f32)
    num=jnp.sum(jnp.where((tcol==lanef)&(lane<32),1.0,0.0),axis=0,keepdims=True)
    g=jnp.floor((num+3.0)*0.25)
    start=jnp.sum(jnp.where(lanef<tcol,jnp.broadcast_to(g,(NBP,128)),0.0),axis=1,keepdims=True)
    pos=jnp.where(live,4.0*start+rank,-1.0).astype(jnp.int32)
    ident=iota((NBP,1),0).astype(f32)*64.0+bs_col+1.0
    hit=pos==iota((NBP,NSLOT),1)
    slots=jnp.sum(jnp.where(hit,jnp.broadcast_to(ident,(NBP,NSLOT)),0.0),axis=0,keepdims=True)
    l2=iota((128,128),1); s2=iota((128,128),0)
    gend=jnp.sum(jnp.where(l2<=s2,jnp.broadcast_to(g,(128,128)),0.0),axis=1,keepdims=True)
    gt=jnp.sum(jnp.where((s2<32)&(gend<=l2.astype(f32)),1.0,0.0),axis=0,keepdims=True)
    total=jnp.sum(g,axis=1,keepdims=True)
    return slots, jnp.where(iota((1,128),1)==127,jnp.broadcast_to(total,(1,128)),gt)

def sort_kernel(cnt, packed, plan):
    p=packed[...].astype(f32)
    q=p.T[:,0:1]
    tile=jnp.floor(q*(1.0/64.0))
    slots,gt=sort_blocks(cnt[0],jnp.floor(p[0:1]*(1.0/64.0)),tile,q-64.0*tile)
    plan[0:1]=slots.astype(jnp.int32)
    plan[1:2,0:128]=gt.astype(jnp.int32)

def spread_kernel(obs, weight, prior, w0, wgt, pri):
    pri[...]=jnp.broadcast_to(prior[...],(128,256)).T
    own=pl.multiple_of(8*lax.axis_index("region"),8)
    def spread(x): return jnp.broadcast_to(x,(128,64)).T
    mine=weight[pl.ds(own,8)]
    for k in range(8):
        wgt[k]=spread(mine[k:k+1])
    every=weight[...]
    for k in range(32):
        w0[k]=(spread(every[k:k+1])*obs[k]).astype(bf16)

SM=pl.BlockSpec(memory_space=pltpu.SMEM); VM=pl.BlockSpec(memory_space=pltpu.VMEM)
def begin(cnt, bs, bt, obs, weight, prior):
    packed=jnp.pad((bt*64+bs).reshape(1,NB),((0,7),(0,NBP-NB)))
    plan=pl.pallas_call(sort_kernel,out_shape=SH((2,NSLOT),jnp.int32),in_specs=[SM,VM],out_specs=VM,
        cost_estimate=pl.CostEstimate(flops=10**10,bytes_accessed=3*10**7,transcendentals=0),
        compiler_params=pltpu.CompilerParams(vmem_limit_bytes=8<<20),name="sort")(cnt,packed)
    w0,wgt,pri=pl.pallas_call(spread_kernel,out_shape=(SH((32,64,128),bf16),SH((8,64,128)),SH((256,128))),
        in_specs=[VM]*3,out_specs=(VM,)*3,
        cost_estimate=pl.CostEstimate(flops=10**9,bytes_accessed=4*10**6,transcendentals=0),
        compiler_params=pltpu.CompilerParams(vmem_limit_bytes=8<<20),name="spread")(obs,weight,prior)
    return plan,w0,wgt,pri

def snd(plan,g,k):
    v=plan[0,4*g+k]
    return jnp.where(v==0,32,jnp.bitwise_and(v-1,63))
def group_loop(plan, body):
    turns=(plan[1,127]+(UN-1))//UN
    def turn(i,c):
        body(i)
        return c
    lax.fori_loop(0,turns,turn,0)
def four(plan,F,g):
    out=[]
    for k in range(4):
        v=plan[0,4*g+k]
        out.append(F[lax.shift_right_logical(jnp.maximum(v-1,0),6)])
    return jnp.concatenate(out,axis=0)

def t_kernel(plan, F, w, pa, pb, wt0, wt1, *rest):
    lane=lax.broadcasted_iota(jnp.int32,(128,128),1)
    for p in range(16):
        x=jnp.concatenate([w[2*p],w[2*p+1]],axis=0).astype(f32).T
        y=pltpu.roll(x,64,1)
        lo=lane<64
        z=jnp.zeros_like(x)
        wt0[2*p]=jnp.where(lo,x,z).astype(bf16)
        wt1[2*p]=jnp.where(lo,z,y).astype(bf16)
        wt0[2*p+1]=jnp.where(lo,y,z).astype(bf16)
        wt1[2*p+1]=jnp.where(lo,z,x).astype(bf16)
    wt0[32]=jnp.zeros((128,128),bf16)
    wt1[32]=jnp.zeros((128,128),bf16)
    direct=pa.dtype==f32
    for ref in (pa,pb) if direct else rest: ref[...]=jnp.zeros_like(ref)
    def body(i):
        for j in range(UN):
            g=i*UN+j
            s=[snd(plan,g,k) for k in range(4)]
            lhs=jnp.concatenate([wt0[s[0]]+wt1[s[1]],wt0[s[2]]+wt1[s[3]]],axis=1)
            x=jnp.dot(lhs,four(plan,F,g),preferred_element_type=f32)
            t=jnp.minimum(plan[1,g],31)
            if direct:
                c=jnp.bitwise_and(t,1); z=jnp.bitwise_and(lax.shift_right_logical(t,1),3); y=lax.shift_right_logical(t,3)
                pa[c,z,y]+=x[0:64]
                pb[c,y,z]+=x[64:128]
            else: rest[0][t]+=x
    group_loop(plan,body)
    if not direct:
        for y in range(4):
            for z in range(4):
                for c in range(2):
                    x=rest[0][(y*4+z)*2+c].astype(pa.dtype)
                    pa[c,z,y]=x[0:64]
                    pb[c,y,z]=x[64:128]
def transpose_map(plan, F, w, dtype):
    o=SH((2,4,4,64,256),dtype)
    return pl.pallas_call(t_kernel,out_shape=(o,o),in_specs=[SM,VM,VM],out_specs=(VM,VM),
        scratch_shapes=[pltpu.VMEM((33,128,128),bf16)]*2+([] if dtype==f32 else [pltpu.VMEM((32,128,256),f32)]),
        compiler_params=pltpu.CompilerParams(vmem_limit_bytes=24<<20), name="tmap")(plan,F,w)

def f_kernel(plan, F, va, vb, img, acc):
    acc[...]=jnp.zeros_like(acc)
    def body(i):
        for j in range(UN):
            g=i*UN+j
            t=jnp.minimum(plan[1,g],31)
            c=jnp.bitwise_and(t,1); z=jnp.bitwise_and(lax.shift_right_logical(t,1),3); y=lax.shift_right_logical(t,3)
            rhs=jnp.concatenate([va[c,z*4+y],vb[c,y*4+z]],axis=0)
            out=jnp.dot(four(plan,F,g),rhs,preferred_element_type=f32)
            for k in range(4):
                acc[snd(plan,g,k)]+=out[64*k:64*k+64]
    group_loop(plan,body)
    img[...]=acc[0:32].astype(img.dtype)
def forward_map(plan, F, va, vb):
    return pl.pallas_call(f_kernel,out_shape=SH((32,64,128),bf16),in_specs=[SM,VM,VM,VM],out_specs=VM,
        scratch_shapes=[pltpu.VMEM((33,64,128),f32)],
        compiler_params=pltpu.CompilerParams(vmem_limit_bytes=18<<20), name="fmap")(plan,F,va.reshape(2,16,128,128),vb.reshape(2,16,128,128))

MESH=pl.DeviceIdType.MESH
class Net:
    def __init__(self, send, recv):
        self.send, self.recv, self.ns, self.nr, self.owed = send, recv, 0, 0, []
    def sender(self, whole):
        k=self.ns; self.ns+=1
        self.owed.append((k,whole))
        return k
    def taker(self):
        k=self.nr; self.nr+=1
        return k
    def put(self, src, dst, dev, sk, rk):
        pltpu.make_async_remote_copy(src_ref=src,dst_ref=dst,send_sem=self.send.at[sk],recv_sem=self.recv.at[rk],device_id=dev,device_id_type=MESH).start()
    def take(self, rk, whole):
        pltpu.make_async_copy(whole,whole,self.recv.at[rk]).wait()
    def drain(self):
        for k,whole in self.owed:
            pltpu.make_async_copy(whole,whole,self.send.at[k]).wait()

def place():
    o=lax.axis_index("orbit"); r=lax.axis_index("region")
    return o//8,(o//2)%4,o%2,r
def dev(y,z,c,r): return (y*8+z*2+c, r)
def greet(devs):
    bar=pltpu.get_barrier_semaphore()
    for d in devs:
        pl.semaphore_signal(bar,inc=1,device_id=d,device_id_type=MESH)
    pl.semaphore_wait(bar,len(devs))

class Ring:
    def __init__(self, i, at):
        self.i=i
        self.to=[(i+d)%4 for d in range(4)]
        self.dev=[at((i+d)%4) for d in range(4)]
    def peers(self): return self.dev[1:4]
FAR=(1,3,2)

def reduce_scratch(dt, cdt, relays=0):
    V=pltpu.VMEM
    return [V((4,4,64,256),cdt)]*2+[V((4,4,64,256),dt)]*2+[V((3,4,64,256),dt)]*2+[V((3,64,256),dt)]*4+[V((relays,64,256),dt)]*(4 if relays else 0)

def reduce_tiles(net, mate, c, ry, rz, pa, pb, sc, tick=lambda k:None, relays=0):
    ra,rb,qa,qb,ga,gb,sa,sb,ha,hb=sc[:10]
    ia,ib,oa,ob=sc[10:] if relays else (None,)*4
    sides=((ry,rz,pa,ra,qa,ga,sa,ha),(rz,ry,pb,rb,qb,gb,sb,hb))
    inn=(ia,ib); out=(oa,ob)
    order=(2,1,3,0)
    way=lambda k: 1 if k%2==0 else 3
    s0=[net.sender(r) for (m,n,p,r,q,g,s,h) in sides]
    k0=[[net.taker() for x in sides] for e in order]
    for k,e in enumerate(order):
        for b,(m,n,p,r,q,g,s,h) in enumerate(sides):
            net.put(p.at[1-c,n.to[e]],r.at[n.to[e]],mate,s0[b],k0[k][b])
    tick(0)
    if relays<4: s1=[net.sender(g.at[pl.ds(0,3),pl.ds(0,4-relays)]) for (m,n,p,r,q,g,s,h) in sides]
    k1=[[net.taker() for x in sides] for e in order]
    if relays:
        sr=[net.sender(x) for x in inn]
        sn=[net.sender(g.at[pl.ds(0,2),pl.ds(0,relays)]) for (m,n,p,r,q,g,s,h) in sides]
        kr=[[net.taker() for x in sides] for k in range(relays)]
    for k,e in enumerate(order):
        for b,(m,n,p,r,q,g,s,h) in enumerate(sides):
            j=n.to[e]
            net.take(k0[k][b],r.at[j])
            for d in (2,4-way(k),way(k)) if k<relays else FAR:
                q[j,m.to[d]]=(p[c,j,m.to[d]].astype(f32)+r[j,m.to[d]].astype(f32)).astype(q.dtype)
                if k>=relays: net.put(q.at[j,m.to[d]],g.at[d-1,j],m.dev[d],s1[b],k1[k][b])
                elif d==2: net.put(q.at[j,m.to[d]],inn[b].at[k],m.dev[way(k)],sr[b],kr[k][b])
                elif d!=way(k): net.put(q.at[j,m.to[d]],g.at[d-1,j],m.dev[d],sn[b],k1[k][b])
    for k in range(relays):
        for b,(m,n,p,r,q,g,s,h) in enumerate(sides):
            j=n.to[order[k]]; w=way(k)
            net.take(kr[k][b],inn[b].at[k])
            out[b][k]=(q[j,m.to[w]].astype(f32)+inn[b][k].astype(f32)).astype(q.dtype)
            net.put(out[b].at[k],g.at[w-1,j],m.dev[w],sn[b],k1[k][b])
    tick(1)
    s2=[net.sender(s) for (m,n,p,r,q,g,s,h) in sides]
    k2=[net.taker() for x in sides]
    own=[None,None]
    for k,e in enumerate(order):
        for b,(m,n,p,r,q,g,s,h) in enumerate(sides):
            j=n.to[e]
            x=p[c,j,m.i].astype(f32)+r[j,m.i].astype(f32)
            if k<relays:
                net.take(k1[k][b],h.at[pl.ds(0,2)])
                x=x+(g[0,j].astype(f32)+g[2,j].astype(f32))
            else:
                net.take(k1[k][b],h)
                x=x+(g[0,j].astype(f32)+g[1,j].astype(f32)+g[2,j].astype(f32))
            if e:
                s[e-1]=x.astype(s.dtype)
                net.put(s.at[e-1],h.at[e-1],n.dev[e],s2[b],k2[b])
            else: own[b]=x
    tick(2)
    for b,(m,n,p,r,q,g,s,h) in enumerate(sides):
        net.take(k2[b],h)
        own[b]=own[b]+(h[0].astype(f32)+h[1].astype(f32)+h[2].astype(f32))
    return jnp.concatenate(own,axis=0)

def gather_tiles(net, mate, c, ry, rz, va, vb, tick=lambda k:None):
    sides=((ry,rz,va),(rz,ry,vb))
    three=[v.at[0,0,pl.ds(0,3)] for m,n,v in sides]
    s1=[net.sender(x) for x in three]
    k1=[[net.taker() for d in range(3)] for x in sides]
    for b,(m,n,v) in enumerate(sides):
        s=v.at[c,n.i,m.i]
        for d in (1,3,2): net.put(s,s,n.dev[d],s1[b],k1[b][d-1])
    tick(0)
    s2=[net.sender(v.at[0,pl.ds(0,3)]) for m,n,v in sides]
    order=(0,3,1,2)
    k2=[[net.taker() for x in sides] for e in order]
    for k,e in enumerate(order):
        for b,(m,n,v) in enumerate(sides):
            s=v.at[c,n.to[e],m.i]
            if e: net.take(k1[b][3-e],s)
            for d in FAR: net.put(s,s,m.dev[d],s2[b],k2[k][b])
    tick(1)
    s3=[net.sender(v.at[0]) for m,n,v in sides]
    k3=[net.taker() for x in sides]
    for k,e in enumerate(order):
        for b,(m,n,v) in enumerate(sides):
            net.take(k2[k][b],three[b])
            s=v.at[c,n.to[e]]
            net.put(s,s,mate,s3[b],k3[b])
        if k==1: tick(2)
    tick(3)
    for b,(m,n,v) in enumerate(sides): net.take(k3[b],v.at[0])

class Reduce:
    def __init__(self, net, sin, sout, axes, base=0):
        self.net, self.sin, self.sout, self.axes = net, sin, sout, axes
        self.at=base; self.so=base; self.k=0
    def start(self, value):
        self.value=value
        self._send()
    def _send(self):
        a=self.axes[self.k]
        self.sout[self.so]=self.value
        sk=self.net.sender(self.sin.at[pl.ds(self.at,len(a))]); self.rk=self.net.taker()
        for i,d in enumerate(a): self.net.put(self.sout.at[self.so],self.sin.at[self.at+i],d,sk,self.rk)
    def step(self):
        n=len(self.axes[self.k])
        self.net.take(self.rk,self.sin.at[pl.ds(self.at,n)])
        for i in range(n): self.value=self.value+self.sin[self.at+i]
        self.at+=n; self.so+=1; self.k+=1
        if self.k<len(self.axes): self._send()
    def finish(self):
        while self.k<len(self.axes): self.step()
        return self.value
def rep(v): return jnp.broadcast_to(v,(8,128))

def first_kernel(pa, pb, prior, r0, va, vb, npl, *s):
    sc=s[:-4]; sin,sout,ssem,rsem=s[-4:]
    y,z,c,r=place(); mate=dev(y,z,1-c,r)
    ry=Ring(y,lambda i:dev(i,z,c,r)); rz=Ring(z,lambda i:dev(y,i,c,r))
    greet([mate]+ry.peers()+rz.peers())
    net=Net(ssem,rsem)
    t=reduce_tiles(net,mate,c,ry,rz,pa,pb,sc,relays=RELAYS)
    res=prior[...]*t.T
    v=(prior[...]*res).astype(bf16)
    va[c,z,y]=v[0:128]; vb[c,y,z]=v[128:256]
    red=Reduce(net,sin,sout,[ry.peers(),rz.peers(),[mate]])
    def tick(k):
        if k==0:
            r0[...]=res
            red.start(rep(jnp.sum(res*res,axis=0,keepdims=True)))
        elif k>1: red.step()
    gather_tiles(net,mate,c,ry,rz,va,vb,tick)
    npl[...]=red.finish()
    net.drain()
    assert (net.ns,net.nr)==FIRST_NET, (net.ns,net.nr)

def mid_kernel(pa, pb, prior, r0, nrm, wi, r1, it, va, vb, two, *s):
    sc=s[:-4]; sin,sout,ssem,rsem=s[-4:]
    y,z,c,r=place(); mate=dev(y,z,1-c,r)
    ry=Ring(y,lambda i:dev(i,z,c,r)); rz=Ring(z,lambda i:dev(y,i,c,r))
    greet([mate]+ry.peers()+rz.peers())
    net=Net(ssem,rsem)
    plane=[ry.peers(),rz.peers(),[mate]]
    ra=Reduce(net,sin,sout,plane,0)
    def tick(k):
        if k==0: ra.start(wi[...])
        else: ra.step()
    t=reduce_tiles(net,mate,c,ry,rz,pa,pb,sc,tick)
    n0=nrm[0:1]
    step=n0/(n0+ra.finish()[0:1])
    d0=r0[...]
    res=d0-step*(d0+prior[...]*t.T)
    v=(prior[...]*res).astype(bf16)
    va[c,z,y]=v[0:128]; vb[c,y,z]=v[128:256]
    rc=Reduce(net,sin,sout,plane,7)
    def tick2(k):
        if k==0:
            it[...]=step*d0
            r1[...]=res
            first_row=lax.broadcasted_iota(jnp.int32,(8,128),0)==0
            rc.start(jnp.where(first_row,rep(jnp.sum(res*res,axis=0,keepdims=True)),rep(jnp.sum(res*d0,axis=0,keepdims=True))))
        elif k>1: rc.step()
    gather_tiles(net,mate,c,ry,rz,va,vb,tick2)
    two[...]=rc.finish()
    net.drain()
    assert (net.ns,net.nr)==MID_NET, (net.ns,net.nr)

def last_kernel(pa, pb, top, low, wi, back, step, *s):
    sc=s[:-4]; sin,sout,ssem,rsem=s[-4:]
    y,z,c,r=place(); mate=dev(y,z,1-c,r)
    ry=Ring(y,lambda i:dev(i,z,c,r)); rz=Ring(z,lambda i:dev(y,i,c,r))
    greet([mate]+ry.peers()+rz.peers())
    net=Net(ssem,rsem)
    ra=Reduce(net,sin,sout,[ry.peers(),rz.peers(),[mate]],0)
    def tick(k):
        if k==0: ra.start(wi[...])
        else: ra.step()
    t=reduce_tiles(net,mate,c,ry,rz,pa,pb,sc,tick)
    step[...]=top[...]/(low[...]+ra.finish())
    back[...]=t.T
    net.drain()
    assert (net.ns,net.nr)==LAST_NET, (net.ns,net.nr)

CH=4
def exchange(img, wgt, w, sin, sout, ssem, rsem, g, part, keep, base):
    y,z,c,r=place()
    rx=Ring(r,lambda i:dev(y,z,c,i))
    greet(rx.peers())
    net=Net(ssem,rsem)
    n=8//CH
    B=[pl.ds(j*n,n) for j in range(CH)]
    s1=net.sender(g); k1=[net.taker() for j in range(CH)]
    ra=Reduce(net,sin,sout,[rx.peers()],0)
    ra.start(part)
    for j in range(CH):
        for d in FAR: net.put(img.at[rx.to[d],B[j]],g.at[d-1,B[j]],rx.dev[d],s1,k1[j])
    sums=jnp.zeros((64,128),f32)
    s2=net.sender(g); k2=net.taker()
    extra=base(ra.finish())
    for j in range(CH):
        b=B[j]
        x=img[r,b].astype(f32)
        net.take(k1[j],g.at[pl.ds(0,3),pl.ds(0,n)])
        x=extra(b,x+(g[0,b].astype(f32)+g[1,b].astype(f32)+g[2,b].astype(f32)))
        keep(b,x)
        m=wgt[b]*x
        w[r,b]=m.astype(bf16)
        s=w.at[r,b]
        for d in FAR: net.put(s,s,rx.dev[d],s2,k2)
        sums=sums+jnp.sum(m*x,axis=0)
    rb=Reduce(net,sin,sout,[rx.peers()],3)
    rb.start(rep(jnp.sum(sums,axis=0,keepdims=True)))
    wi=rb.finish()
    net.take(k2,g)
    net.drain()
    assert (net.ns,net.nr)==CROSS_NET, (net.ns,net.nr)
    return wi

def cross_kernel(img, wgt, part, w, tot, wi, image, g, sin, sout, ssem, rsem):
    def base(total):
        tot[...]=total
        return lambda b,x: x
    def keep(b,x): image[b]=x
    wi[...]=exchange(img,wgt,w,sin,sout,ssem,rsem,g,part[...],keep,base)

def again_kernel(img, wgt, part, n0, image, w, low, top, beta, wi, g, sin, sout, ssem, rsem):
    def base(total):
        n1=total[0:1]
        ratio=n1/n0[0:1]
        top[...]=rep(n1)
        beta[...]=rep(ratio)
        low[...]=rep(n1+ratio*(2.0*total[1:2]+ratio*n0[0:1]))
        return lambda b,x: x+ratio*image[b]
    wi[...]=exchange(img,wgt,w,sin,sout,ssem,rsem,g,part[...],lambda b,x:None,base)

RELAYS=4; FIRST_NET=(17,45); MID_NET=(18,40); LAST_NET=(9,21); CROSS_NET=(4,CH+3)
def _call(kernel, outs, scratch, cid, lim, name, *args):
    return pl.pallas_call(kernel,out_shape=outs,in_specs=[VM]*len(args),out_specs=tuple([VM]*len(outs)),
        scratch_shapes=scratch,compiler_params=pltpu.CompilerParams(collective_id=cid,has_side_effects=True,vmem_limit_bytes=lim<<20),name=name)(*args)
VA=SH((2,4,4,128,128),bf16); ROW=SH((8,128)); TILE=SH((256,128))
def tail(n, net): return [pltpu.VMEM((n,8,128),f32)]*2+[pltpu.SemaphoreType.DMA((k,)) for k in net]
def first(pa,pb,prior):
    return _call(first_kernel,[TILE,VA,VA,ROW],reduce_scratch(f32,f32,RELAYS)+tail(7,FIRST_NET),0,22,"first",pa,pb,prior)
def mid(pa,pb,prior,r0,nrm,wi):
    return _call(mid_kernel,[TILE,TILE,VA,VA,ROW],reduce_scratch(bf16,pa.dtype)+tail(14,MID_NET),1,18,"mid",pa,pb,prior,r0,nrm,wi)
def last(pa,pb,top,low,wi):
    return _call(last_kernel,[TILE,ROW],reduce_scratch(bf16,pa.dtype)+tail(7,LAST_NET),2,14,"last",pa,pb,top,low,wi)
def cross(img,wgt,part):
    return _call(cross_kernel,[SH((4,8,64,128),bf16),ROW,ROW,SH((8,64,128))],[pltpu.VMEM((3,8,64,128),bf16)]+tail(6,CROSS_NET),3,8,"cross",img.reshape(4,8,64,128),wgt,part)
def again(img,wgt,part,n0,image):
    return _call(again_kernel,[SH((4,8,64,128),bf16),ROW,ROW,ROW,ROW],[pltpu.VMEM((3,8,64,128),bf16)]+tail(6,CROSS_NET),4,8,"again",img.reshape(4,8,64,128),wgt,part,n0,image)

def per_device(footprints, block_sounding, block_tile, block_count, observations, obs_weight, prior_std):
    F = footprints
    plan, w0, wgt, prior = begin(block_count, block_sounding, block_tile, observations, obs_weight, prior_std.reshape(1, 256))
    pa, pb = transpose_map(plan, F, w0, f32)
    r0, va, vb, norm = first(pa, pb, prior)
    img = forward_map(plan, F, va, vb)
    w, norm, wi, image = cross(img, wgt, norm)
    pa, pb = transpose_map(plan, F, w.reshape(32, 64, 128), f32)
    r1, it, va, vb, two = mid(pa, pb, prior, r0, norm, wi)
    img = forward_map(plan, F, va, vb)
    w, low, top, beta, wi = again(img, wgt, two, norm, image)
    pa, pb = transpose_map(plan, F, w.reshape(32, 64, 128), bf16)
    back, step = last(pa, pb, top, low, wi)
    step, beta = step[0:1], beta[0:1]
    d1 = r1 + beta * r0
    resid = r1 - step * (d1 + prior * back)
    flux = prior * (it + step * d1)
    return flux[None, None], resid[None, None]


def solution(mesh):
    return jax.shard_map(
        per_device,
        mesh=mesh,
        in_specs=(
            P(("orbit", "region"), None, None),
            P(("orbit", "region")),
            P(("orbit", "region")),
            P(("orbit", "region")),
            P("orbit", None, None),
            P("orbit", None),
            P("region", "orbit", None),
        ),
        out_specs=(P("region", "orbit", None, None), P("region", "orbit", None, None)),
        check_vma=False,
    )
```

```python
import jax
import jax.numpy as jnp
from jax import lax
from jax.experimental import pallas as pl
from jax.experimental.pallas import tpu as pltpu
from jax.sharding import PartitionSpec as P

f32 = jnp.float32
bf16 = jnp.bfloat16
def SH(shape, dtype=f32): return jax.ShapeDtypeStruct(shape, dtype)

NB=320; NBP=384; NSLOT=512; UN=24; NCH=4

def sort_blocks(n, bt_row, bt_col, bs_col):
    iota=lambda shape,d: lax.broadcasted_iota(jnp.int32, shape, d)
    trow=jnp.where(iota((1,NBP),1)<n, bt_row, 32.0)
    live=iota((NBP,1),0)<n
    tcol=jnp.where(live, bt_col, 32.0)
    same=(trow==tcol)&(iota((NBP,NBP),1)<iota((NBP,NBP),0))
    rank=jnp.sum(jnp.where(same,1.0,0.0),axis=1,keepdims=True)
    lane=iota((NBP,128),1); lanef=lane.astype(f32)
    num=jnp.sum(jnp.where((tcol==lanef)&(lane<32),1.0,0.0),axis=0,keepdims=True)
    g=jnp.floor((num+3.0)*0.25)
    start=jnp.sum(jnp.where(lanef<tcol,jnp.broadcast_to(g,(NBP,128)),0.0),axis=1,keepdims=True)
    pos=jnp.where(live,4.0*start+rank,-1.0).astype(jnp.int32)
    ident=iota((NBP,1),0).astype(f32)*64.0+bs_col+1.0
    hit=pos==iota((NBP,NSLOT),1)
    slots=jnp.sum(jnp.where(hit,jnp.broadcast_to(ident,(NBP,NSLOT)),0.0),axis=0,keepdims=True)
    l2=iota((128,128),1); s2=iota((128,128),0)
    gend=jnp.sum(jnp.where(l2<=s2,jnp.broadcast_to(g,(128,128)),0.0),axis=1,keepdims=True)
    gt=jnp.sum(jnp.where((s2<32)&(gend<=l2.astype(f32)),1.0,0.0),axis=0,keepdims=True)
    total=jnp.sum(g,axis=1,keepdims=True)
    return slots, jnp.where(iota((1,128),1)==127,jnp.broadcast_to(total,(1,128)),gt)

def sort_kernel(cnt, packed, plan):
    p=packed[...].astype(f32)
    q=p.T[:,0:1]
    tile=jnp.floor(q*(1.0/64.0))
    slots,gt=sort_blocks(cnt[0],jnp.floor(p[0:1]*(1.0/64.0)),tile,q-64.0*tile)
    plan[0:1]=slots.astype(jnp.int32)
    plan[1:2,0:128]=gt.astype(jnp.int32)

def spread_kernel(obs, weight, prior, w0, wgt, pri):
    pri[...]=jnp.broadcast_to(prior[...],(128,256)).T
    own=pl.multiple_of(8*lax.axis_index("region"),8)
    def spread(x): return jnp.broadcast_to(x,(128,64)).T
    mine=weight[pl.ds(own,8)]
    for k in range(8):
        wgt[k]=spread(mine[k:k+1])
    every=weight[...]
    for k in range(32):
        w0[k]=(spread(every[k:k+1])*obs[k]).astype(bf16)

SM=pl.BlockSpec(memory_space=pltpu.SMEM); VM=pl.BlockSpec(memory_space=pltpu.VMEM)
def begin(cnt, bs, bt, obs, weight, prior):
    packed=jnp.pad((bt*64+bs).reshape(1,NB),((0,7),(0,NBP-NB)))
    plan=pl.pallas_call(sort_kernel,out_shape=SH((2,NSLOT),jnp.int32),in_specs=[SM,VM],out_specs=VM,
        cost_estimate=pl.CostEstimate(flops=10**10,bytes_accessed=3*10**7,transcendentals=0),
        compiler_params=pltpu.CompilerParams(vmem_limit_bytes=8<<20),name="sort")(cnt,packed)
    w0,wgt,pri=pl.pallas_call(spread_kernel,out_shape=(SH((32,64,128),bf16),SH((8,64,128)),SH((256,128))),
        in_specs=[VM]*3,out_specs=(VM,)*3,
        cost_estimate=pl.CostEstimate(flops=10**9,bytes_accessed=4*10**6,transcendentals=0),
        compiler_params=pltpu.CompilerParams(vmem_limit_bytes=8<<20),name="spread")(obs,weight,prior)
    return plan,w0,wgt,pri

def snd(plan,g,k):
    v=plan[0,4*g+k]
    return jnp.where(v==0,32,jnp.bitwise_and(v-1,63))
def group_loop(plan, body):
    turns=(plan[1,127]+(UN-1))//UN
    def turn(i,c):
        body(i)
        return c
    lax.fori_loop(0,turns,turn,0)
def four(plan,F,g):
    out=[]
    for k in range(4):
        v=plan[0,4*g+k]
        out.append(F[lax.shift_right_logical(jnp.maximum(v-1,0),6)])
    return jnp.concatenate(out,axis=0)

def t_kernel(plan, F, w, pa, pb, acc, wt0, wt1):
    lane=lax.broadcasted_iota(jnp.int32,(128,128),1)
    for p in range(16):
        x=jnp.concatenate([w[2*p],w[2*p+1]],axis=0).astype(f32).T
        y=pltpu.roll(x,64,1)
        lo=lane<64
        z=jnp.zeros_like(x)
        wt0[2*p]=jnp.where(lo,x,z).astype(bf16)
        wt1[2*p]=jnp.where(lo,z,y).astype(bf16)
        wt0[2*p+1]=jnp.where(lo,y,z).astype(bf16)
        wt1[2*p+1]=jnp.where(lo,z,x).astype(bf16)
    wt0[32]=jnp.zeros((128,128),bf16)
    wt1[32]=jnp.zeros((128,128),bf16)
    acc[...]=jnp.zeros_like(acc)
    def body(i):
        for j in range(UN):
            g=i*UN+j
            s=[snd(plan,g,k) for k in range(4)]
            lhs=jnp.concatenate([wt0[s[0]]+wt1[s[1]],wt0[s[2]]+wt1[s[3]]],axis=1)
            acc[plan[1,g]]+=jnp.dot(lhs,four(plan,F,g),preferred_element_type=f32)
    group_loop(plan,body)
    for y in range(4):
        for z in range(4):
            for c in range(2):
                x=acc[(y*4+z)*2+c].astype(pa.dtype)
                pa[c,z,y]=x[0:64]
                pb[c,y,z]=x[64:128]
def transpose_map(plan, F, w, dtype):
    o=SH((2,4,4,64,256),dtype)
    return pl.pallas_call(t_kernel,out_shape=(o,o),in_specs=[SM,VM,VM],out_specs=(VM,VM),
        scratch_shapes=[pltpu.VMEM((33,128,256),f32),pltpu.VMEM((33,128,128),bf16),pltpu.VMEM((33,128,128),bf16)],
        compiler_params=pltpu.CompilerParams(vmem_limit_bytes=24<<20), name="tmap")(plan,F,w)

def f_kernel(plan, F, va, vb, img, acc):
    acc[...]=jnp.zeros_like(acc)
    def body(i):
        for j in range(UN):
            g=i*UN+j
            t=jnp.minimum(plan[1,g],31)
            c=jnp.bitwise_and(t,1); z=jnp.bitwise_and(lax.shift_right_logical(t,1),3); y=lax.shift_right_logical(t,3)
            rhs=jnp.concatenate([va[c,z*4+y],vb[c,y*4+z]],axis=0)
            out=jnp.dot(four(plan,F,g),rhs,preferred_element_type=f32)
            for k in range(4):
                acc[snd(plan,g,k)]+=out[64*k:64*k+64]
    group_loop(plan,body)
    img[...]=acc[0:32].astype(img.dtype)
def forward_map(plan, F, va, vb):
    return pl.pallas_call(f_kernel,out_shape=SH((32,64,128),bf16),in_specs=[SM,VM,VM,VM],out_specs=VM,
        scratch_shapes=[pltpu.VMEM((33,64,128),f32)],
        compiler_params=pltpu.CompilerParams(vmem_limit_bytes=18<<20), name="fmap")(plan,F,va.reshape(2,16,128,128),vb.reshape(2,16,128,128))

MESH=pl.DeviceIdType.MESH
class Net:
    def __init__(self, send, recv):
        self.send, self.recv, self.ns, self.nr, self.owed = send, recv, 0, 0, []
    def sender(self, whole):
        k=self.ns; self.ns+=1
        self.owed.append((k,whole))
        return k
    def taker(self):
        k=self.nr; self.nr+=1
        return k
    def put(self, src, dst, dev, sk, rk):
        pltpu.make_async_remote_copy(src_ref=src,dst_ref=dst,send_sem=self.send.at[sk],recv_sem=self.recv.at[rk],device_id=dev,device_id_type=MESH).start()
    def take(self, rk, whole):
        pltpu.make_async_copy(whole,whole,self.recv.at[rk]).wait()
    def drain(self):
        for k,whole in self.owed:
            pltpu.make_async_copy(whole,whole,self.send.at[k]).wait()

def place():
    o=lax.axis_index("orbit"); r=lax.axis_index("region")
    return o//8,(o//2)%4,o%2,r
def dev(y,z,c,r): return (y*8+z*2+c, r)
def greet(devs):
    bar=pltpu.get_barrier_semaphore()
    for d in devs:
        pl.semaphore_signal(bar,inc=1,device_id=d,device_id_type=MESH)
    pl.semaphore_wait(bar,len(devs))

class Ring:
    def __init__(self, i, at):
        self.i=i
        self.to=[(i+d)%4 for d in range(4)]
        self.dev=[at((i+d)%4) for d in range(4)]
    def peers(self): return self.dev[1:4]
FAR=(1,3,2)

def reduce_scratch(dt, cdt, relays=0):
    V=pltpu.VMEM
    return [V((4,4,64,256),cdt)]*2+[V((4,4,64,256),dt)]*2+[V((3,4,64,256),dt)]*2+[V((3,64,256),dt)]*4+[V((relays,64,256),dt)]*(4 if relays else 0)

def reduce_tiles(net, mate, c, ry, rz, pa, pb, sc, tick=lambda k:None, relays=0):
    ra,rb,qa,qb,ga,gb,sa,sb,ha,hb=sc[:10]
    ia,ib,oa,ob=sc[10:] if relays else (None,)*4
    sides=((ry,rz,pa,ra,qa,ga,sa,ha),(rz,ry,pb,rb,qb,gb,sb,hb))
    inn=(ia,ib); out=(oa,ob)
    order=(2,1,3,0)
    way=lambda k: 1 if k%2==0 else 3
    s0=[net.sender(r) for (m,n,p,r,q,g,s,h) in sides]
    k0=[[net.taker() for x in sides] for e in order]
    for k,e in enumerate(order):
        for b,(m,n,p,r,q,g,s,h) in enumerate(sides):
            net.put(p.at[1-c,n.to[e]],r.at[n.to[e]],mate,s0[b],k0[k][b])
    tick(0)
    if relays<4: s1=[net.sender(g.at[pl.ds(0,3),pl.ds(0,4-relays)]) for (m,n,p,r,q,g,s,h) in sides]
    k1=[[net.taker() for x in sides] for e in order]
    if relays:
        sr=[net.sender(x) for x in inn]
        sn=[net.sender(g.at[pl.ds(0,2),pl.ds(0,relays)]) for (m,n,p,r,q,g,s,h) in sides]
        kr=[[net.taker() for x in sides] for k in range(relays)]
    for k,e in enumerate(order):
        for b,(m,n,p,r,q,g,s,h) in enumerate(sides):
            j=n.to[e]
            net.take(k0[k][b],r.at[j])
            for d in (2,4-way(k),way(k)) if k<relays else FAR:
                q[j,m.to[d]]=(p[c,j,m.to[d]].astype(f32)+r[j,m.to[d]].astype(f32)).astype(q.dtype)
                if k>=relays: net.put(q.at[j,m.to[d]],g.at[d-1,j],m.dev[d],s1[b],k1[k][b])
                elif d==2: net.put(q.at[j,m.to[d]],inn[b].at[k],m.dev[way(k)],sr[b],kr[k][b])
                elif d!=way(k): net.put(q.at[j,m.to[d]],g.at[d-1,j],m.dev[d],sn[b],k1[k][b])
    for k in range(relays):
        for b,(m,n,p,r,q,g,s,h) in enumerate(sides):
            j=n.to[order[k]]; w=way(k)
            net.take(kr[k][b],inn[b].at[k])
            out[b][k]=(q[j,m.to[w]].astype(f32)+inn[b][k].astype(f32)).astype(q.dtype)
            net.put(out[b].at[k],g.at[w-1,j],m.dev[w],sn[b],k1[k][b])
    tick(1)
    s2=[net.sender(s) for (m,n,p,r,q,g,s,h) in sides]
    k2=[net.taker() for x in sides]
    own=[None,None]
    for k,e in enumerate(order):
        for b,(m,n,p,r,q,g,s,h) in enumerate(sides):
            j=n.to[e]
            x=p[c,j,m.i].astype(f32)+r[j,m.i].astype(f32)
            if k<relays:
                net.take(k1[k][b],h.at[pl.ds(0,2)])
                x=x+(g[0,j].astype(f32)+g[2,j].astype(f32))
            else:
                net.take(k1[k][b],h)
                x=x+(g[0,j].astype(f32)+g[1,j].astype(f32)+g[2,j].astype(f32))
            if e:
                s[e-1]=x.astype(s.dtype)
                net.put(s.at[e-1],h.at[e-1],n.dev[e],s2[b],k2[b])
            else: own[b]=x
    tick(2)
    for b,(m,n,p,r,q,g,s,h) in enumerate(sides):
        net.take(k2[b],h)
        own[b]=own[b]+(h[0].astype(f32)+h[1].astype(f32)+h[2].astype(f32))
    return jnp.concatenate(own,axis=0)

def gather_tiles(net, mate, c, ry, rz, va, vb, tick=lambda k:None):
    sides=((ry,rz,va),(rz,ry,vb))
    three=[v.at[0,0,pl.ds(0,3)] for m,n,v in sides]
    s1=[net.sender(x) for x in three]
    k1=[[net.taker() for d in range(3)] for x in sides]
    for b,(m,n,v) in enumerate(sides):
        s=v.at[c,n.i,m.i]
        for d in (1,3,2): net.put(s,s,n.dev[d],s1[b],k1[b][d-1])
    tick(0)
    s2=[net.sender(v.at[0,pl.ds(0,3)]) for m,n,v in sides]
    order=(0,3,1,2)
    k2=[[net.taker() for x in sides] for e in order]
    for k,e in enumerate(order):
        for b,(m,n,v) in enumerate(sides):
            s=v.at[c,n.to[e],m.i]
            if e: net.take(k1[b][3-e],s)
            for d in FAR: net.put(s,s,m.dev[d],s2[b],k2[k][b])
    tick(1)
    s3=[net.sender(v.at[0]) for m,n,v in sides]
    k3=[net.taker() for x in sides]
    for k,e in enumerate(order):
        for b,(m,n,v) in enumerate(sides):
            net.take(k2[k][b],three[b])
            s=v.at[c,n.to[e]]
            net.put(s,s,mate,s3[b],k3[b])
        if k==1: tick(2)
    tick(3)
    for b,(m,n,v) in enumerate(sides): net.take(k3[b],v.at[0])

class Reduce:
    def __init__(self, net, sin, sout, axes, base=0):
        self.net, self.sin, self.sout, self.axes = net, sin, sout, axes
        self.at=base; self.so=base; self.k=0
    def start(self, value):
        self.value=value
        self._send()
    def _send(self):
        a=self.axes[self.k]
        self.sout[self.so]=self.value
        sk=self.net.sender(self.sin.at[pl.ds(self.at,len(a))]); self.rk=self.net.taker()
        for i,d in enumerate(a): self.net.put(self.sout.at[self.so],self.sin.at[self.at+i],d,sk,self.rk)
    def step(self):
        n=len(self.axes[self.k])
        self.net.take(self.rk,self.sin.at[pl.ds(self.at,n)])
        for i in range(n): self.value=self.value+self.sin[self.at+i]
        self.at+=n; self.so+=1; self.k+=1
        if self.k<len(self.axes): self._send()
    def finish(self):
        while self.k<len(self.axes): self.step()
        return self.value
def rep(v): return jnp.broadcast_to(v,(8,128))

def first_kernel(pa, pb, prior, r0, va, vb, npl, *s):
    sc=s[:-4]; sin,sout,ssem,rsem=s[-4:]
    y,z,c,r=place(); mate=dev(y,z,1-c,r)
    ry=Ring(y,lambda i:dev(i,z,c,r)); rz=Ring(z,lambda i:dev(y,i,c,r))
    greet([mate]+ry.peers()+rz.peers())
    net=Net(ssem,rsem)
    t=reduce_tiles(net,mate,c,ry,rz,pa,pb,sc,relays=RELAYS)
    res=prior[...]*t.T
    v=(prior[...]*res).astype(bf16)
    va[c,z,y]=v[0:128]; vb[c,y,z]=v[128:256]
    red=Reduce(net,sin,sout,[ry.peers(),rz.peers(),[mate]])
    def tick(k):
        if k==0:
            r0[...]=res
            red.start(rep(jnp.sum(res*res,axis=0,keepdims=True)))
        elif k>1: red.step()
    gather_tiles(net,mate,c,ry,rz,va,vb,tick)
    npl[...]=red.finish()
    net.drain()
    assert (net.ns,net.nr)==FIRST_NET, (net.ns,net.nr)

def mid_kernel(pa, pb, prior, r0, nrm, wi, r1, it, va, vb, two, *s):
    sc=s[:-4]; sin,sout,ssem,rsem=s[-4:]
    y,z,c,r=place(); mate=dev(y,z,1-c,r)
    ry=Ring(y,lambda i:dev(i,z,c,r)); rz=Ring(z,lambda i:dev(y,i,c,r))
    greet([mate]+ry.peers()+rz.peers())
    net=Net(ssem,rsem)
    plane=[ry.peers(),rz.peers(),[mate]]
    ra=Reduce(net,sin,sout,plane,0)
    def tick(k):
        if k==0: ra.start(wi[...])
        else: ra.step()
    t=reduce_tiles(net,mate,c,ry,rz,pa,pb,sc,tick)
    n0=nrm[0:1]
    step=n0/(n0+ra.finish()[0:1])
    d0=r0[...]
    res=d0-step*(d0+prior[...]*t.T)
    v=(prior[...]*res).astype(bf16)
    va[c,z,y]=v[0:128]; vb[c,y,z]=v[128:256]
    rc=Reduce(net,sin,sout,plane,7)
    def tick2(k):
        if k==0:
            it[...]=step*d0
            r1[...]=res
            first_row=lax.broadcasted_iota(jnp.int32,(8,128),0)==0
            rc.start(jnp.where(first_row,rep(jnp.sum(res*res,axis=0,keepdims=True)),rep(jnp.sum(res*d0,axis=0,keepdims=True))))
        elif k>1: rc.step()
    gather_tiles(net,mate,c,ry,rz,va,vb,tick2)
    two[...]=rc.finish()
    net.drain()
    assert (net.ns,net.nr)==MID_NET, (net.ns,net.nr)

def last_kernel(pa, pb, top, low, wi, back, step, *s):
    sc=s[:-4]; sin,sout,ssem,rsem=s[-4:]
    y,z,c,r=place(); mate=dev(y,z,1-c,r)
    ry=Ring(y,lambda i:dev(i,z,c,r)); rz=Ring(z,lambda i:dev(y,i,c,r))
    greet([mate]+ry.peers()+rz.peers())
    net=Net(ssem,rsem)
    ra=Reduce(net,sin,sout,[ry.peers(),rz.peers(),[mate]],0)
    def tick(k):
        if k==0: ra.start(wi[...])
        else: ra.step()
    t=reduce_tiles(net,mate,c,ry,rz,pa,pb,sc,tick)
    step[...]=top[...]/(low[...]+ra.finish())
    back[...]=t.T
    net.drain()
    assert (net.ns,net.nr)==LAST_NET, (net.ns,net.nr)

CH=4
def exchange(img, wgt, w, sin, sout, ssem, rsem, g, part, keep, base):
    y,z,c,r=place()
    rx=Ring(r,lambda i:dev(y,z,c,i))
    greet(rx.peers())
    net=Net(ssem,rsem)
    n=8//CH
    B=[pl.ds(j*n,n) for j in range(CH)]
    s1=net.sender(g); k1=[net.taker() for j in range(CH)]
    ra=Reduce(net,sin,sout,[rx.peers()],0)
    ra.start(part)
    for j in range(CH):
        for d in FAR: net.put(img.at[rx.to[d],B[j]],g.at[d-1,B[j]],rx.dev[d],s1,k1[j])
    sums=jnp.zeros((64,128),f32)
    s2=net.sender(g); k2=net.taker()
    extra=base(ra.finish())
    for j in range(CH):
        b=B[j]
        x=img[r,b].astype(f32)
        net.take(k1[j],g.at[pl.ds(0,3),pl.ds(0,n)])
        x=extra(b,x+(g[0,b].astype(f32)+g[1,b].astype(f32)+g[2,b].astype(f32)))
        keep(b,x)
        m=wgt[b]*x
        w[r,b]=m.astype(bf16)
        s=w.at[r,b]
        for d in FAR: net.put(s,s,rx.dev[d],s2,k2)
        sums=sums+jnp.sum(m*x,axis=0)
    rb=Reduce(net,sin,sout,[rx.peers()],3)
    rb.start(rep(jnp.sum(sums,axis=0,keepdims=True)))
    wi=rb.finish()
    net.take(k2,g)
    net.drain()
    assert (net.ns,net.nr)==CROSS_NET, (net.ns,net.nr)
    return wi

def cross_kernel(img, wgt, part, w, tot, wi, image, g, sin, sout, ssem, rsem):
    def base(total):
        tot[...]=total
        return lambda b,x: x
    def keep(b,x): image[b]=x
    wi[...]=exchange(img,wgt,w,sin,sout,ssem,rsem,g,part[...],keep,base)

def again_kernel(img, wgt, part, n0, image, w, low, top, beta, wi, g, sin, sout, ssem, rsem):
    def base(total):
        n1=total[0:1]
        ratio=n1/n0[0:1]
        top[...]=rep(n1)
        beta[...]=rep(ratio)
        low[...]=rep(n1+ratio*(2.0*total[1:2]+ratio*n0[0:1]))
        return lambda b,x: x+ratio*image[b]
    wi[...]=exchange(img,wgt,w,sin,sout,ssem,rsem,g,part[...],lambda b,x:None,base)

RELAYS=4; FIRST_NET=(17,45); MID_NET=(18,40); LAST_NET=(9,21); CROSS_NET=(4,CH+3)
def _call(kernel, outs, scratch, cid, lim, name, *args):
    return pl.pallas_call(kernel,out_shape=outs,in_specs=[VM]*len(args),out_specs=tuple([VM]*len(outs)),
        scratch_shapes=scratch,compiler_params=pltpu.CompilerParams(collective_id=cid,has_side_effects=True,vmem_limit_bytes=lim<<20),name=name)(*args)
VA=SH((2,4,4,128,128),bf16); ROW=SH((8,128)); TILE=SH((256,128))
def tail(n, net): return [pltpu.VMEM((n,8,128),f32)]*2+[pltpu.SemaphoreType.DMA((k,)) for k in net]
def first(pa,pb,prior):
    return _call(first_kernel,[TILE,VA,VA,ROW],reduce_scratch(f32,f32,RELAYS)+tail(7,FIRST_NET),0,22,"first",pa,pb,prior)
def mid(pa,pb,prior,r0,nrm,wi):
    return _call(mid_kernel,[TILE,TILE,VA,VA,ROW],reduce_scratch(bf16,pa.dtype)+tail(14,MID_NET),1,18,"mid",pa,pb,prior,r0,nrm,wi)
def last(pa,pb,top,low,wi):
    return _call(last_kernel,[TILE,ROW],reduce_scratch(bf16,pa.dtype)+tail(7,LAST_NET),2,14,"last",pa,pb,top,low,wi)
def cross(img,wgt,part):
    return _call(cross_kernel,[SH((4,8,64,128),bf16),ROW,ROW,SH((8,64,128))],[pltpu.VMEM((3,8,64,128),bf16)]+tail(6,CROSS_NET),3,8,"cross",img.reshape(4,8,64,128),wgt,part)
def again(img,wgt,part,n0,image):
    return _call(again_kernel,[SH((4,8,64,128),bf16),ROW,ROW,ROW,ROW],[pltpu.VMEM((3,8,64,128),bf16)]+tail(6,CROSS_NET),4,8,"again",img.reshape(4,8,64,128),wgt,part,n0,image)

def per_device(footprints, block_sounding, block_tile, block_count, observations, obs_weight, prior_std):
    F = footprints
    plan, w0, wgt, prior = begin(block_count, block_sounding, block_tile, observations, obs_weight, prior_std.reshape(1, 256))
    pa, pb = transpose_map(plan, F, w0, f32)
    r0, va, vb, norm = first(pa, pb, prior)
    img = forward_map(plan, F, va, vb)
    w, norm, wi, image = cross(img, wgt, norm)
    pa, pb = transpose_map(plan, F, w.reshape(32, 64, 128), bf16)
    r1, it, va, vb, two = mid(pa, pb, prior, r0, norm, wi)
    img = forward_map(plan, F, va, vb)
    w, low, top, beta, wi = again(img, wgt, two, norm, image)
    pa, pb = transpose_map(plan, F, w.reshape(32, 64, 128), bf16)
    back, step = last(pa, pb, top, low, wi)
    step, beta = step[0:1], beta[0:1]
    d1 = r1 + beta * r0
    resid = r1 - step * (d1 + prior * back)
    flux = prior * (it + step * d1)
    return flux[None, None], resid[None, None]


def solution(mesh):
    return jax.shard_map(
        per_device,
        mesh=mesh,
        in_specs=(
            P(("orbit", "region"), None, None),
            P(("orbit", "region")),
            P(("orbit", "region")),
            P(("orbit", "region")),
            P("orbit", None, None),
            P("orbit", None),
            P("region", "orbit", None),
        ),
        out_specs=(P("region", "orbit", None, None), P("region", "orbit", None, None)),
        check_vma=False,
    )
```
